32 devices in a mesh: ia: 2 (over y), ja: 4 (over x, core), ka: 4 (over z).
Axes of the slice: x: 2, y: 2, z: 4, core: 2. Of those that a mesh axis runs over, the one named last changes fastest.
Arguments:
- tensor: float32 [32, 256, 8192], P('ia', 'ka', 'ja'), may hold values from -6 to 6
- factor_b: float32 [8192, 64], P(('ja', 'ka')), may hold values from -1 to 1
- factor_c: float32 [256, 64], P('ka'), may hold values from -1 to 1
Outputs:
- factor_a: float32 [32, 64], P(('ia', 'ja', 'ka'))
- mode_two: float32 [64, 4, 2048], P(None, 'ja', ('ia', 'ka'))
The draws below stay inside these ranges and needn't reach their ends.
All inputs are finite; a program needn't handle non-finite values.
Results may differ from the reference program's by a relative error of at most 0.00026.
Values sent between devices are 32-bit elements; how exact they have to be, the bound alone decides.
No kernel may reach another device: no remote copies, remote signals or barrier semaphores. Data moves between devices by JAX's collectives and lax.ppermute only.
A program may use at most 64 MiB of HBM per device.

```python
import jax
import jax.numpy as jnp
from jax import lax

R = 64
J_DEV = 2048
I = 32
J = 8192
K = 256
N_JA = 4


def common_factor(key, row_total):
    first_key, second_key = jax.random.split(key, 2)
    shared = jax.random.normal(first_key, (row_total, 1), jnp.float32)
    noise = jax.random.normal(second_key, (row_total, R), jnp.float32)
    values = jnp.clip(shared + noise, -8.0, 8.0) / jnp.sqrt(jnp.float32(row_total))
    return jnp.clip(values, -1.0, 1.0)


def draw_factor_b(key, part):
    return common_factor(jax.random.fold_in(key, 11), J)


def draw_factor_c(key, part):
    return common_factor(jax.random.fold_in(key, 23), K)


def level_of(own_key, extent, cuts, smallest, largest):
    factor_of, own = 1.0, jax.random.fold_in(own_key, 6)
    for axis_at, blocks in cuts:
        steps = jnp.exp(jax.random.uniform(jax.random.fold_in(own, axis_at), (blocks,), jnp.float32, smallest / len(cuts), largest / len(cuts)))
        factor_of = factor_of * jnp.repeat(steps, extent[axis_at] // blocks).reshape([-1 if axis == axis_at else 1 for axis in range(len(extent))])
    return factor_of


def scatter_about(own_key, extent, deviation, most, cuts=(), kind=jnp.bfloat16):
    result = deviation * jax.random.normal(own_key, extent, jnp.float32)
    if cuts:
        result = result * level_of(own_key, extent, cuts, -0.22, 0.18)
    return jnp.clip(result, -most, most).astype(kind)


def setup_inputs(seed: int = 0) -> dict:
    key_list = jax.random.split(jax.random.key(seed), 4)
    return {
        "tensor": scatter_about(key_list[0], (I, K, J), 1.0, 6.0, ((0, 2), (1, 4), (2, 4)), jnp.float32),
        "factor_b": draw_factor_b(jax.random.fold_in(key_list[3], 71), 0),
        "factor_c": draw_factor_c(jax.random.fold_in(key_list[3], 71), 0),
    }


def reference(tensor, factor_b, factor_c):
    highest = lax.Precision.HIGHEST
    gram_b = jnp.dot(factor_b.T.astype(jnp.float32), factor_b.astype(jnp.float32), precision=highest, preferred_element_type=jnp.float32)
    gram_c = jnp.dot(factor_c.T.astype(jnp.float32), factor_c.astype(jnp.float32), precision=highest, preferred_element_type=jnp.float32)
    triangle = jnp.linalg.cholesky(gram_b * gram_c)

    def mode_one_row(snapshot_rows):
        contracted = jnp.dot(factor_c.T.astype(jnp.float32), snapshot_rows.astype(jnp.float32), precision=highest, preferred_element_type=jnp.float32)
        return jnp.sum(contracted * factor_b.T, axis=1)
    mode_one = lax.map(mode_one_row, tensor)
    factor_a = jax.scipy.linalg.cho_solve((triangle, True), mode_one.T).T

    def accumulate(running, scan_items):
        snapshot_rows, a_row = scan_items
        contracted = jnp.dot(factor_c.T.astype(jnp.float32), snapshot_rows.astype(jnp.float32), precision=highest, preferred_element_type=jnp.float32)
        return (running + contracted * a_row[:, None], None)
    empty_sum = jnp.zeros((factor_c.shape[1], tensor.shape[2]), jnp.float32)
    mode_two, _ = lax.scan(accumulate, empty_sum, (tensor, factor_a))
    return (factor_a, mode_two.reshape(factor_c.shape[1], N_JA, J_DEV))
```

```python
import functools

import jax
import jax.numpy as jnp
from jax import lax
from jax.experimental import pallas as pl
from jax.experimental.pallas import tpu as pltpu
from jax.sharding import PartitionSpec as P


F32 = jnp.float32
BF16 = jnp.bfloat16
HIGHEST = lax.Precision.HIGHEST
LANES = 128
SUBLANES = 8
VMEM = pl.BlockSpec(memory_space=pltpu.VMEM)
NN = (((1,), (0,)), ((), ()))
NT = (((1,), (1,)), ((), ()))
TN = (((0,), (0,)), ((), ()))


def dot(a, b, dims):
    return lax.dot_general(a, b, dims, precision=HIGHEST, preferred_element_type=F32)


def pinned(x):
    return pltpu.with_memory_space_constraint(x, pltpu.VMEM)


def cost(flops, bytes_accessed):
    return pl.CostEstimate(flops=flops, bytes_accessed=bytes_accessed, transcendentals=0)


def pack_kernel(bt_ref, c_ref, out_ref):
    rank, width = bt_ref.shape
    out_ref[:rank, :] = bt_ref[...]
    groups = width // rank
    out_ref[rank:, :] = jnp.concatenate(
        [c_ref[SUBLANES * g : SUBLANES * (g + 1), :] for g in range(groups)], axis=1
    )


def contract_kernel(x_ref, c_ref, q_ref, lhs_ref, *, rows):
    step = pl.program_id(0)

    @pl.when(step == 0)
    def _():
        ct = c_ref[...].T
        high = ct.astype(BF16)
        low = (ct - high.astype(F32)).astype(BF16)
        lhs_ref[...] = jnp.concatenate([high, low, high, low], axis=1)

    for row in range(rows):
        x = x_ref[row]
        high = x.astype(BF16)
        low = (x - high.astype(F32)).astype(BF16)
        rhs = jnp.concatenate([high, high, low, low], axis=0)
        q_ref[step * rows + row] = jnp.dot(lhs_ref[...], rhs, preferred_element_type=F32)


def contract(tensor, factor_c):
    row_block, depth, width = tensor.shape
    rank = factor_c.shape[1]
    rows = 2
    return pl.pallas_call(
        functools.partial(contract_kernel, rows=rows),
        grid=(row_block // rows,),
        out_shape=pltpu.VMEM((row_block, rank, width), F32),
        in_specs=[
            pl.BlockSpec((rows, depth, width), lambda g: (g, 0, 0)),
            VMEM,
        ],
        out_specs=VMEM,
        scratch_shapes=[pltpu.VMEM((rank, 4 * depth), BF16)],
        compiler_params=pltpu.CompilerParams(vmem_limit_bytes=16 << 20),
        cost_estimate=cost(8 * row_block * depth * rank * width, 4 * row_block * depth * width),
        name="contract",
    )(tensor, factor_c)


def mode_one_kernel(q_ref, *refs):
    part_refs, (out_ref, sums_ref) = refs[:-2], refs[-2:]
    row_block, rank, _ = q_ref.shape
    width = part_refs[0].shape[1]
    here = lax.axis_index("ka")
    gram = jnp.zeros((rank, rank), F32)
    for part in part_refs:
        value = part[:rank, :]
        gram = gram + dot(value, value, NT)
    for tile in range(rank // SUBLANES):
        rows = pl.ds(tile * SUBLANES, SUBLANES)
        for i in range(row_block):
            total = jnp.zeros((SUBLANES, LANES), F32)
            for s, part in enumerate(part_refs):
                start = (here ^ s) * width
                for c in range(0, width, LANES):
                    columns = pl.ds(pl.multiple_of(start + c, LANES), LANES)
                    total = total + q_ref[i, rows, columns] * part[rows, c : c + LANES]
            sums_ref[i * rank + tile * SUBLANES : i * rank + (tile + 1) * SUBLANES, :] = total
    flat = dot(jnp.ones((SUBLANES, LANES), F32), sums_ref[...], NT)
    lines = row_block * rank // LANES
    line = lax.broadcasted_iota(jnp.int32, (lines, LANES), 0)
    packed = jnp.zeros((lines, LANES), F32)
    for v in range(lines):
        packed = jnp.where(line == v, flat[:, v * LANES : (v + 1) * LANES], packed)
    half = rank // 2
    out_ref[:half, :] = jnp.concatenate([gram[:half, :], gram[half:, :]], axis=1)
    out_ref[half:, :] = packed


def mode_one_sums(q, parts):
    row_block, rank, width = q.shape
    lines = row_block * rank // LANES
    return pl.pallas_call(
        mode_one_kernel,
        out_shape=jax.ShapeDtypeStruct((rank // 2 + lines, LANES), F32),
        in_specs=[VMEM] * (1 + len(parts)),
        out_specs=VMEM,
        scratch_shapes=[pltpu.VMEM((row_block * rank, LANES), F32)],
        compiler_params=pltpu.CompilerParams(vmem_limit_bytes=16 << 20),
        cost_estimate=cost(2 * row_block * rank * width, 4 * row_block * rank * width),
        name="mode_one",
    )(pinned(q), *parts)


def add_kernel(*refs):
    part_refs, out_ref = refs[:-1], refs[-1]
    lines = out_ref.shape[0]
    first = part_refs[0].shape[0] - lines
    total = part_refs[0][first:, :]
    for part in part_refs[1:]:
        total = total + part[first:, :]
    out_ref[...] = total


def add_tail(parts, lines):
    return pl.pallas_call(
        add_kernel,
        out_shape=jax.ShapeDtypeStruct((lines, LANES), F32),
        in_specs=[VMEM] * len(parts),
        out_specs=VMEM,
        compiler_params=pltpu.CompilerParams(vmem_limit_bytes=4 << 20),
        name="add_tail",
    )(*parts)


def spd_inverse(matrix):
    n = matrix.shape[0]
    row = lax.broadcasted_iota(jnp.int32, (n, n), 0)
    column = lax.broadcasted_iota(jnp.int32, (n, n), 1)
    work = jnp.concatenate([matrix, jnp.where(row == column, 1.0, 0.0).astype(F32)], axis=1)
    wide_row = lax.broadcasted_iota(jnp.int32, (n, 2 * n), 0)
    for k in range(0, n, 4):
        c = [jnp.broadcast_to(work[:, k + q : k + q + 1], (n, 2 * n)) for q in range(4)]
        a = [jnp.broadcast_to(work[k + q : k + q + 1, :], (SUBLANES, 2 * n)) for q in range(4)]
        p = [
            [jnp.broadcast_to(c[s][k + q : k + q + 1, :], (SUBLANES, 2 * n)) for s in range(4)]
            for q in range(4)
        ]
        scale = 1.0 / (p[0][0] * p[1][1] - p[0][1] * p[1][0])
        r0 = (p[1][1] * a[0] - p[0][1] * a[1]) * scale
        r1 = (p[0][0] * a[1] - p[1][0] * a[0]) * scale
        u02 = (p[1][1] * p[0][2] - p[0][1] * p[1][2]) * scale
        u12 = (p[0][0] * p[1][2] - p[1][0] * p[0][2]) * scale
        u03 = (p[1][1] * p[0][3] - p[0][1] * p[1][3]) * scale
        u13 = (p[0][0] * p[1][3] - p[1][0] * p[0][3]) * scale
        s22 = p[2][2] - p[2][0] * u02 - p[2][1] * u12
        s23 = p[2][3] - p[2][0] * u03 - p[2][1] * u13
        s32 = p[3][2] - p[3][0] * u02 - p[3][1] * u12
        s33 = p[3][3] - p[3][0] * u03 - p[3][1] * u13
        b2 = a[2] - p[2][0] * r0 - p[2][1] * r1
        b3 = a[3] - p[3][0] * r0 - p[3][1] * r1
        scale = 1.0 / (s22 * s33 - s23 * s32)
        r2 = (s33 * b2 - s23 * b3) * scale
        r3 = (s22 * b3 - s32 * b2) * scale
        r0 = r0 - u02 * r2 - u03 * r3
        r1 = r1 - u12 * r2 - u13 * r3
        r = [jnp.broadcast_to(v[:1, :], (n, 2 * n)) for v in (r0, r1, r2, r3)]
        updated = work - c[0] * r[0] - c[1] * r[1] - c[2] * r[2] - c[3] * r[3]
        for q in range(4):
            updated = jnp.where(wide_row == k + q, r[q], updated)
        work = updated
    return work[:, n:]


def inverse_kernel(*refs):
    out_ref = refs[-1]
    count = (len(refs) - 1) // 2
    gram_refs, part_refs = refs[:count], refs[count:-1]
    rank = out_ref.shape[0]
    half = rank // 2
    folded = gram_refs[0][:half, :]
    for ref in gram_refs[1:]:
        folded = folded + ref[:half, :]
    gram_b = jnp.concatenate([folded[:, :rank], folded[:, rank:]], axis=0)
    rows = []
    for ref in part_refs:
        tail = ref[rank:, :]
        rows += [tail[:, g * rank : (g + 1) * rank] for g in range(tail.shape[1] // rank)]
    c_rows = jnp.concatenate(rows, axis=0)
    gram_c = dot(c_rows, c_rows, TN)
    out_ref[...] = spd_inverse(gram_b * gram_c)


def inverse(grams, parts):
    rank = grams[0].shape[1] // 2
    return pl.pallas_call(
        inverse_kernel,
        out_shape=jax.ShapeDtypeStruct((rank, rank), F32),
        in_specs=[VMEM] * (len(grams) + len(parts)),
        out_specs=VMEM,
        compiler_params=pltpu.CompilerParams(vmem_limit_bytes=8 << 20),
        cost_estimate=cost(4000000, 4000000),
        name="inverse",
    )(*grams, *parts)


def mode_two_kernel(q_ref, inv_ref, *refs):
    sum_refs, (a_ref, keep_ref, send_ref) = refs[:-3], refs[-3:]
    row_block, rank, width = q_ref.shape
    half = width // 2
    lines = row_block * rank // LANES
    packed = sum_refs[0][...]
    for ref in sum_refs[1:]:
        packed = packed + ref[...]
    rows = jnp.concatenate([packed[:, :rank], packed[:, rank:]], axis=0)
    inv = inv_ref[...]
    a_rows = dot(rows, inv, NT)
    a_cols = dot(inv, rows, NT)
    mine = lax.axis_index("ja") * lax.axis_size("ka") + lax.axis_index("ka")
    place = (mine % 2) * lines + mine // 2
    row = lax.broadcasted_iota(jnp.int32, (row_block, rank), 0)
    a_ref[...] = jnp.sum(jnp.where(row == place, a_rows, 0.0), axis=0, keepdims=True)
    here = lax.axis_index("ia") % 2
    for out_ref, start in ((send_ref, (1 - here) * half), (keep_ref, here * half)):
        for tile in range(rank // SUBLANES):
            rs = pl.ds(tile * SUBLANES, SUBLANES)
            factors = []
            for i in range(row_block):
                at = (i % 2) * lines + i // 2
                factors.append(
                    jnp.broadcast_to(
                        a_cols[tile * SUBLANES : (tile + 1) * SUBLANES, at : at + 1],
                        (SUBLANES, LANES),
                    )
                )
            for c in range(0, half, LANES):
                columns = pl.ds(pl.multiple_of(start + c, LANES), LANES)
                total = factors[0] * q_ref[0, rs, columns]
                for i in range(1, row_block):
                    total = total + factors[i] * q_ref[i, rs, columns]
                out_ref[rs, c : c + LANES] = total


def mode_two_sums(q, inv, sums):
    row_block, rank, width = q.shape
    half = width // 2
    return pl.pallas_call(
        mode_two_kernel,
        out_shape=(
            jax.ShapeDtypeStruct((1, rank), F32),
            jax.ShapeDtypeStruct((rank, half), F32),
            jax.ShapeDtypeStruct((rank, half), F32),
        ),
        in_specs=[VMEM] * (2 + len(sums)),
        out_specs=[VMEM] * 3,
        compiler_params=pltpu.CompilerParams(vmem_limit_bytes=16 << 20),
        cost_estimate=cost(2 * row_block * rank * width, 4 * row_block * rank * width),
        name="mode_two",
    )(pinned(q), inv, *sums)


def split_kernel(keep_ref, got_ref, *out_refs):
    here = lax.axis_index("ka")
    width = out_refs[0].shape[1]
    for s, out_ref in enumerate(out_refs):
        columns = pl.ds(pl.multiple_of((here ^ s) * width, LANES), width)
        out_ref[...] = keep_ref[:, columns] + got_ref[:, columns]


def split_sums(keep, got, count):
    rank, half = keep.shape
    return pl.pallas_call(
        split_kernel,
        out_shape=[jax.ShapeDtypeStruct((rank, half // count), F32)] * count,
        in_specs=[VMEM] * 2,
        out_specs=[VMEM] * count,
        compiler_params=pltpu.CompilerParams(vmem_limit_bytes=8 << 20),
        name="split_sums",
    )(keep, got)


def final_kernel(*refs):
    part_refs, out_ref = refs[:-1], refs[-1]
    total = part_refs[0][...]
    for ref in part_refs[1:]:
        total = total + ref[...]
    out_ref[:, 0, :] = total


def final_sum(parts):
    rank, width = parts[0].shape
    return pl.pallas_call(
        final_kernel,
        out_shape=jax.ShapeDtypeStruct((rank, 1, width), F32),
        in_specs=[VMEM] * len(parts),
        out_specs=VMEM,
        compiler_params=pltpu.CompilerParams(vmem_limit_bytes=8 << 20),
        name="final_sum",
    )(*parts)


def swap(x, axis, s):
    n = lax.axis_size(axis)
    return lax.ppermute(x, axis, [(i, i ^ s) for i in range(n)])


def swaps(x, axis):
    n = lax.axis_size(axis)
    got = {s: swap(x, axis, s) for s in reversed(range(1, n))}
    return [x] + [got[s] for s in range(1, n)]


def body(tensor, factor_b, factor_c):
    row_block, depth, width = tensor.shape
    rank = factor_c.shape[1]
    n_ia, n_ka = lax.axis_size("ia"), lax.axis_size("ka")
    lines = row_block * rank // LANES
    packed = pl.pallas_call(
        pack_kernel,
        out_shape=jax.ShapeDtypeStruct((rank + SUBLANES, factor_b.shape[0]), F32),
        in_specs=[VMEM] * 2,
        out_specs=VMEM,
        compiler_params=pltpu.CompilerParams(vmem_limit_bytes=4 << 20),
        name="pack",
    )(factor_b.T, factor_c)
    parts = swaps(packed, "ka")
    q = contract(tensor, factor_c)
    sums = swaps(mode_one_sums(q, parts), "ja")
    tail = add_tail(sums, lines)
    tails = swaps(tail, "ka")
    inv = inverse(sums, parts)
    a_row, keep, send = mode_two_sums(q, inv, tails)
    if n_ia == 2 and keep.shape[1] % (n_ka * LANES) == 0:
        got = swap(send, "ia", 1)
        pieces = split_sums(keep, got, n_ka)
        final = [pieces[0]] + [swap(pieces[s], "ka", s) for s in reversed(range(1, n_ka))]
        return a_row, final_sum(final)
    whole = jnp.where(
        lax.axis_index("ia") % 2 == 0,
        jnp.concatenate([keep, send], axis=1),
        jnp.concatenate([send, keep], axis=1),
    )
    reduced = lax.psum_scatter(whole, ("ia", "ka"), scatter_dimension=1, tiled=True)
    return a_row, reduced.reshape(rank, 1, reduced.shape[1])


def solution(mesh):
    placed = (P("ia", "ka", "ja"), P(("ja", "ka"), None), P("ka", None))
    return jax.shard_map(
        body,
        mesh=mesh,
        in_specs=placed,
        out_specs=(P(("ia", "ja", "ka"), None), P(None, "ja", ("ia", "ka"))),
        check_vma=False,
    )
```

```python
import functools

import jax
import jax.numpy as jnp
from jax import lax
from jax.experimental import pallas as pl
from jax.experimental.pallas import tpu as pltpu
from jax.sharding import PartitionSpec as P


F32 = jnp.float32
BF16 = jnp.bfloat16
HIGHEST = lax.Precision.HIGHEST
LANES = 128
SUBLANES = 8
VMEM = pl.BlockSpec(memory_space=pltpu.VMEM)
NN = (((1,), (0,)), ((), ()))
NT = (((1,), (1,)), ((), ()))
TN = (((0,), (0,)), ((), ()))


def dot(a, b, dims):
    return lax.dot_general(a, b, dims, precision=HIGHEST, preferred_element_type=F32)


def cost(flops, bytes_accessed):
    return pl.CostEstimate(flops=flops, bytes_accessed=bytes_accessed, transcendentals=0)


def placed_in(x, space):
    return pltpu.with_memory_space_constraint(x, space)


def fold(square):
    half = square.shape[0] // 2
    return jnp.concatenate([square[:half, :], square[half:, :]], axis=1)


def unfold(folded):
    half = folded.shape[1] // 2
    return jnp.concatenate([folded[:, :half], folded[:, half:]], axis=0)


def total_of(refs, start=0, stop=None):
    total = refs[0][start:stop, :]
    for ref in refs[1:]:
        total = total + ref[start:stop, :]
    return total


def contract_kernel(x_ref, c_ref, q_ref, gram_ref, lhs_ref, *, rows):
    step = pl.program_id(0)

    @pl.when(step == 0)
    def _():
        c = c_ref[...]
        gram_ref[...] = fold(dot(c, c, TN))
        ct = c.T
        high = ct.astype(BF16)
        low = (ct - high.astype(F32)).astype(BF16)
        lhs_ref[...] = jnp.concatenate([high, low, high, low], axis=1)

    for row in range(rows):
        x = x_ref[row]
        high = x.astype(BF16)
        low = (x - high.astype(F32)).astype(BF16)
        rhs = jnp.concatenate([high, high, low, low], axis=0)
        q_ref[step * rows + row] = jnp.dot(lhs_ref[...], rhs, preferred_element_type=F32)


def contract(tensor, factor_c):
    row_block, depth, width = tensor.shape
    rank = factor_c.shape[1]
    rows = 2
    return pl.pallas_call(
        functools.partial(contract_kernel, rows=rows),
        grid=(row_block // rows,),
        out_shape=(
            pltpu.VMEM((row_block, rank, width), F32),
            jax.ShapeDtypeStruct((rank // 2, 2 * rank), F32),
        ),
        in_specs=[
            pl.BlockSpec((rows, depth, width), lambda g: (g, 0, 0)),
            pl.BlockSpec((depth, rank), lambda g: (0, 0)),
        ],
        out_specs=[VMEM, VMEM],
        scratch_shapes=[pltpu.VMEM((rank, 4 * depth), BF16)],
        compiler_params=pltpu.CompilerParams(vmem_limit_bytes=16 << 20),
        cost_estimate=cost(8 * row_block * depth * rank * width, 4 * row_block * depth * width),
        name="contract",
    )(placed_in(tensor, pltpu.HBM), placed_in(factor_c, pltpu.HBM))


def mode_one_kernel(q_ref, *refs):
    part_refs, out_ref = refs[:-1], refs[-1]
    row_block, rank, _ = q_ref.shape
    width = part_refs[0].shape[1]
    here = lax.axis_index("ka")
    lines = out_ref.shape[0] - rank // 2
    lane = lax.broadcasted_iota(jnp.int32, (SUBLANES, LANES), 1)
    packed = [jnp.zeros((SUBLANES, LANES), F32) for _ in range(lines // SUBLANES)]
    for tile in range(rank // SUBLANES):
        rows = pl.ds(tile * SUBLANES, SUBLANES)
        for i in range(row_block):
            total = None
            for s, part in enumerate(part_refs):
                start = (here ^ s) * width
                for c in range(0, width, LANES):
                    columns = pl.ds(pl.multiple_of(start + c, LANES), LANES)
                    term = q_ref[i, rows, columns] * part[rows, c : c + LANES]
                    total = term if total is None else total + term
            group, place = divmod(tile * row_block + i, LANES)
            packed[group] = jnp.where(
                lane == place, jnp.sum(total, axis=1, keepdims=True), packed[group]
            )
    for group, value in enumerate(packed):
        start = rank // 2 + group * SUBLANES
        out_ref[start : start + SUBLANES, :] = value
    stacks = []
    for part in part_refs:
        value = part[...]
        first = value.astype(BF16)
        value = value - first.astype(F32)
        second = value.astype(BF16)
        third = (value - second.astype(F32)).astype(BF16)
        stacks.append(jnp.concatenate([first, second, third], axis=0))
    stack = jnp.concatenate(stacks, axis=1)
    terms = lax.dot_general(stack, stack, NT, preferred_element_type=F32)
    terms = terms[:, 2 * rank :] + terms[:, rank : 2 * rank] + terms[:, :rank]
    gram = terms[2 * rank :, :] + terms[rank : 2 * rank, :] + terms[:rank, :]
    out_ref[: rank // 2, :] = fold(gram)


def mode_one_sums(q, parts):
    row_block, rank, width = q.shape
    lines = row_block * rank // LANES
    return pl.pallas_call(
        mode_one_kernel,
        out_shape=jax.ShapeDtypeStruct((rank // 2 + lines, LANES), F32),
        in_specs=[VMEM] * (1 + len(parts)),
        out_specs=VMEM,
        compiler_params=pltpu.CompilerParams(vmem_limit_bytes=16 << 20),
        cost_estimate=cost(2 * row_block * rank * width, 4 * row_block * rank * width),
        name="mode_one",
    )(placed_in(q, pltpu.VMEM), *parts)


def add_kernel(*refs):
    part_refs, out_ref = refs[:-1], refs[-1]
    out_ref[...] = total_of(part_refs, part_refs[0].shape[0] - out_ref.shape[0])


def add_tail(parts, lines):
    return pl.pallas_call(
        add_kernel,
        out_shape=jax.ShapeDtypeStruct((lines, LANES), F32),
        in_specs=[VMEM] * len(parts),
        out_specs=VMEM,
        compiler_params=pltpu.CompilerParams(vmem_limit_bytes=4 << 20),
        name="add_tail",
    )(*parts)


def solve_rows(pivot, rows):
    count = len(rows)
    rows = list(rows)
    block = {(q, s): pivot[q][s] for q in range(count) for s in range(q, count)}
    upper = {}
    for m in range(0, count, 2):
        a, b, d = block[m, m], block[m, m + 1], block[m + 1, m + 1]
        scale = 1.0 / (a * d - b * b)
        a, b, d = a * scale, b * scale, d * scale
        rows[m], rows[m + 1] = d * rows[m] - b * rows[m + 1], a * rows[m + 1] - b * rows[m]
        for s in range(m + 2, count):
            v, w = block[m, s], block[m + 1, s]
            upper[m, s], upper[m + 1, s] = d * v - b * w, a * w - b * v
        for q in range(m + 2, count):
            v, w = block[m, q], block[m + 1, q]
            for s in range(q, count):
                block[q, s] = block[q, s] - (v * upper[m, s] + w * upper[m + 1, s])
            rows[q] = rows[q] - (v * rows[m] + w * rows[m + 1])
    for m in range(count - 4, -1, -2):
        for s in range(m + 2, count):
            rows[m] = rows[m] - upper[m, s] * rows[s]
            rows[m + 1] = rows[m + 1] - upper[m + 1, s] * rows[s]
    return rows


def spd_inverse(matrix):
    n = matrix.shape[0]
    row = lax.broadcasted_iota(jnp.int32, (n, n), 0)
    column = lax.broadcasted_iota(jnp.int32, (n, n), 1)
    wide = jnp.concatenate([matrix, jnp.where(row == column, 1.0, 0.0).astype(F32)], axis=1)
    shape = (SUBLANES, 2 * n)
    tiles = [wide[t * SUBLANES : (t + 1) * SUBLANES, :] for t in range(n // SUBLANES)]
    sublane = lax.broadcasted_iota(jnp.int32, shape, 0)
    for k, block in enumerate(tiles):
        block = tiles[k]
        at = k * SUBLANES
        columns = [
            [jnp.broadcast_to(tile[:, at + q : at + q + 1], shape) for q in range(SUBLANES)]
            for tile in tiles
        ]
        rows = [jnp.broadcast_to(block[q : q + 1, :], shape) for q in range(SUBLANES)]
        pivot = [
            [jnp.broadcast_to(columns[k][s][q : q + 1, :], shape) for s in range(SUBLANES)]
            for q in range(SUBLANES)
        ]
        rows = solve_rows(pivot, rows)
        updated = []
        for t, tile in enumerate(tiles):
            if t == k:
                value = rows[0]
                for q in range(1, SUBLANES):
                    value = jnp.where(sublane == q, rows[q], value)
            else:
                value = tile
                for q in range(SUBLANES):
                    value = value - columns[t][q] * rows[q]
            updated.append(value)
        tiles = updated
    return jnp.concatenate([tile[:, n:] for tile in tiles], axis=0)


def inverse_kernel(*refs):
    out_ref = refs[-1]
    count = (len(refs) - 1) // 2
    half = out_ref.shape[0] // 2
    gram_b = total_of(refs[:count], 0, half)
    gram_c = total_of(refs[count:-1])
    out_ref[...] = spd_inverse(unfold(gram_b * gram_c))


def inverse(grams_b, grams_c):
    rank = grams_b[0].shape[1] // 2
    return pl.pallas_call(
        inverse_kernel,
        out_shape=jax.ShapeDtypeStruct((rank, rank), F32),
        in_specs=[VMEM] * (len(grams_b) + len(grams_c)),
        out_specs=VMEM,
        compiler_params=pltpu.CompilerParams(vmem_limit_bytes=8 << 20),
        cost_estimate=cost(4000000, 4000000),
        name="inverse",
    )(*grams_b, *grams_c)


def weigh(q_ref, factors, out_ref, start):
    row_block, rank, _ = q_ref.shape
    width = out_ref.shape[1]
    for tile in range(rank // SUBLANES):
        rows = pl.ds(tile * SUBLANES, SUBLANES)
        weights = [
            jnp.broadcast_to(
                factors[tile * SUBLANES : (tile + 1) * SUBLANES, i : i + 1], (SUBLANES, LANES)
            )
            for i in range(row_block)
        ]
        for c in range(0, width, LANES):
            columns = pl.ds(pl.multiple_of(start + c, LANES), LANES)
            total = weights[0] * q_ref[0, rows, columns]
            for i in range(1, row_block):
                total = total + weights[i] * q_ref[i, rows, columns]
            out_ref[rows, c : c + LANES] = total


def send_kernel(q_ref, inv_ref, *refs):
    sum_refs, (a_ref, factors_ref, send_ref) = refs[:-3], refs[-3:]
    row_block, rank, _ = q_ref.shape
    packed = total_of(sum_refs)
    columns = []
    for tile in range(rank // SUBLANES):
        group, place = divmod(tile * row_block, LANES)
        columns.append(
            packed[group * SUBLANES : (group + 1) * SUBLANES, place : place + row_block]
        )
    factors = dot(inv_ref[...], jnp.concatenate(columns, axis=0), NN)
    factors_ref[...] = factors
    weigh(q_ref, factors, send_ref, (1 - lax.axis_index("ia") % 2) * send_ref.shape[1])
    mine = lax.axis_index("ja") * lax.axis_size("ka") + lax.axis_index("ka")
    lane = lax.broadcasted_iota(jnp.int32, (rank, row_block), 1)
    chosen = jnp.where(lane == mine, factors, 0.0)
    a_ref[...] = dot(jnp.ones((SUBLANES, row_block), F32), chosen, NT)[:1, :]


def keep_kernel(q_ref, factors_ref, keep_ref):
    weigh(q_ref, factors_ref[...], keep_ref, (lax.axis_index("ia") % 2) * keep_ref.shape[1])


def mode_two_sums(q, inv, sums):
    row_block, rank, width = q.shape
    half = width // 2
    params = pltpu.CompilerParams(vmem_limit_bytes=16 << 20)
    work = cost(row_block * rank * width, 2 * row_block * rank * width)
    q = placed_in(q, pltpu.VMEM)
    half_shape = jax.ShapeDtypeStruct((rank, half), F32)
    a_row, factors, send = pl.pallas_call(
        send_kernel,
        out_shape=(
            jax.ShapeDtypeStruct((1, rank), F32),
            jax.ShapeDtypeStruct((rank, row_block), F32),
            half_shape,
        ),
        in_specs=[VMEM] * (2 + len(sums)),
        out_specs=[VMEM] * 3,
        compiler_params=params,
        cost_estimate=work,
        name="mode_two_send",
    )(q, inv, *sums)
    keep = pl.pallas_call(
        keep_kernel,
        out_shape=half_shape,
        in_specs=[VMEM] * 2,
        out_specs=VMEM,
        compiler_params=params,
        cost_estimate=work,
        name="mode_two_keep",
    )(q, factors)
    return a_row, keep, send


def split_kernel(keep_ref, got_ref, *out_refs):
    here = lax.axis_index("ka")
    width = out_refs[0].shape[1]
    for s, out_ref in enumerate(out_refs):
        columns = pl.ds(pl.multiple_of((here ^ s) * width, LANES), width)
        out_ref[...] = keep_ref[:, columns] + got_ref[:, columns]


def split_sums(keep, got, count):
    rank, half = keep.shape
    return pl.pallas_call(
        split_kernel,
        out_shape=[jax.ShapeDtypeStruct((rank, half // count), F32)] * count,
        in_specs=[VMEM] * 2,
        out_specs=[VMEM] * count,
        compiler_params=pltpu.CompilerParams(vmem_limit_bytes=8 << 20),
        name="split_sums",
    )(keep, got)


def final_kernel(*refs):
    part_refs, out_ref = refs[:-1], refs[-1]
    total = part_refs[0][...]
    for ref in part_refs[1:]:
        total = total + ref[...]
    out_ref[:, 0, :] = total


def final_sum(parts):
    rank, width = parts[0].shape
    return pl.pallas_call(
        final_kernel,
        out_shape=jax.ShapeDtypeStruct((rank, 1, width), F32),
        in_specs=[VMEM] * len(parts),
        out_specs=VMEM,
        compiler_params=pltpu.CompilerParams(vmem_limit_bytes=8 << 20),
        name="final_sum",
    )(*parts)


def swap(x, axis, s):
    n = lax.axis_size(axis)
    return lax.ppermute(x, axis, [(i, i ^ s) for i in range(n)])


def swaps(x, axis):
    n = lax.axis_size(axis)
    got = {s: swap(x, axis, s) for s in reversed(range(1, n))}
    return [x] + [got[s] for s in range(1, n)]


def body(tensor, factor_b, factor_c):
    row_block, depth, width = tensor.shape
    rank = factor_c.shape[1]
    n_ia, n_ka = lax.axis_size("ia"), lax.axis_size("ka")
    lines = row_block * rank // LANES
    parts = swaps(factor_b.T, "ka")
    q, gram_c = contract(tensor, factor_c)
    grams_c = swaps(gram_c, "ka")
    sums = swaps(mode_one_sums(q, parts), "ja")
    tails = swaps(add_tail(sums, lines), "ka")
    inv = inverse(sums, grams_c)
    a_row, keep, send = mode_two_sums(q, inv, tails)
    if n_ia == 2 and keep.shape[1] % (n_ka * LANES) == 0:
        got = swap(send, "ia", 1)
        pieces = split_sums(keep, got, n_ka)
        final = [pieces[0]] + [swap(pieces[s], "ka", s) for s in reversed(range(1, n_ka))]
        return a_row, final_sum(final)
    whole = jnp.where(
        lax.axis_index("ia") % 2 == 0,
        jnp.concatenate([keep, send], axis=1),
        jnp.concatenate([send, keep], axis=1),
    )
    reduced = lax.psum_scatter(whole, ("ia", "ka"), scatter_dimension=1, tiled=True)
    return a_row, reduced.reshape(rank, 1, reduced.shape[1])


def solution(mesh):
    placed = (P("ia", "ka", "ja"), P(("ja", "ka"), None), P("ka", None))
    return jax.shard_map(
        body,
        mesh=mesh,
        in_specs=placed,
        out_specs=(P(("ia", "ja", "ka"), None), P(None, "ja", ("ia", "ka"))),
        check_vma=False,
    )
```

```python
import functools

import jax
import jax.numpy as jnp
from jax import lax
from jax.experimental import pallas as pl
from jax.experimental.pallas import tpu as pltpu
from jax.sharding import PartitionSpec as P


F32 = jnp.float32
BF16 = jnp.bfloat16
HIGHEST = lax.Precision.HIGHEST
LANES = 128
SUBLANES = 8
VMEM = pl.BlockSpec(memory_space=pltpu.VMEM)
HBM = pl.BlockSpec(memory_space=pltpu.HBM)
NN = (((1,), (0,)), ((), ()))
NT = (((1,), (1,)), ((), ()))
TN = (((0,), (0,)), ((), ()))


def dot(a, b, dims):
    return lax.dot_general(a, b, dims, precision=HIGHEST, preferred_element_type=F32)


def cost(flops, bytes_accessed):
    return pl.CostEstimate(flops=flops, bytes_accessed=bytes_accessed, transcendentals=0)


def placed_in(x, space):
    return pltpu.with_memory_space_constraint(x, space)


def fold(square):
    half = square.shape[0] // 2
    return jnp.concatenate([square[:half, :], square[half:, :]], axis=1)


def unfold(folded):
    half = folded.shape[1] // 2
    return jnp.concatenate([folded[:, :half], folded[:, half:]], axis=0)


def total_of(refs, start=0, stop=None):
    total = refs[0][start:stop, :]
    for ref in refs[1:]:
        total = total + ref[start:stop, :]
    return total


def pack_kernel(bt_hbm, c_hbm, out_ref, c_ref, sems):
    rank, width = bt_hbm.shape
    b_copy = pltpu.make_async_copy(bt_hbm, out_ref.at[pl.ds(0, rank)], sems.at[0])
    c_copy = pltpu.make_async_copy(c_hbm, c_ref, sems.at[1])
    c_copy.start()
    b_copy.start()
    c_copy.wait()
    lines = out_ref.shape[0] - rank
    out_ref[rank:, :] = jnp.concatenate(
        [c_ref[lines * g : lines * (g + 1), :] for g in range(width // rank)], axis=1
    )
    b_copy.wait()


def pack(bt, c):
    rank, width = bt.shape
    lines = c.shape[0] * rank // width
    return pl.pallas_call(
        pack_kernel,
        out_shape=pltpu.VMEM((rank + lines, width), F32),
        in_specs=[HBM, HBM],
        out_specs=VMEM,
        scratch_shapes=[pltpu.VMEM(c.shape, F32), pltpu.SemaphoreType.DMA((2,))],
        compiler_params=pltpu.CompilerParams(vmem_limit_bytes=2 << 20),
        name="pack",
    )(placed_in(bt, pltpu.HBM), placed_in(c, pltpu.HBM))


def contract_kernel(x_hbm, c_hbm, q_ref, x_ref, c_ref, lhs_ref, x_sems, c_sem, *, chunks):
    rows = q_ref.shape[0] // chunks
    copies = [
        pltpu.make_async_copy(
            x_hbm.at[pl.ds(n * rows, rows)], x_ref.at[pl.ds(n * rows, rows)], x_sems.at[n]
        )
        for n in range(chunks)
    ]
    c_copy = pltpu.make_async_copy(c_hbm, c_ref, c_sem)
    c_copy.start()
    for copy in copies:
        copy.start()
    c_copy.wait()
    ct = c_ref[...].T
    high = ct.astype(BF16)
    low = (ct - high.astype(F32)).astype(BF16)
    lhs_ref[...] = jnp.concatenate([high, low, high, low], axis=1)
    for n, copy in enumerate(copies):
        copy.wait()
        for i in range(n * rows, (n + 1) * rows):
            x = x_ref[i]
            high = x.astype(BF16)
            low = (x - high.astype(F32)).astype(BF16)
            rhs = jnp.concatenate([high, high, low, low], axis=0)
            q_ref[i] = jnp.dot(lhs_ref[...], rhs, preferred_element_type=F32)


def contract(tensor, factor_c):
    row_block, depth, width = tensor.shape
    rank = factor_c.shape[1]
    chunks = 4
    return pl.pallas_call(
        functools.partial(contract_kernel, chunks=chunks),
        out_shape=pltpu.VMEM((row_block, rank, width), F32),
        in_specs=[HBM, HBM],
        out_specs=VMEM,
        scratch_shapes=[
            pltpu.VMEM(tensor.shape, F32),
            pltpu.VMEM(factor_c.shape, F32),
            pltpu.VMEM((rank, 4 * depth), BF16),
            pltpu.SemaphoreType.DMA((chunks,)),
            pltpu.SemaphoreType.DMA,
        ],
        compiler_params=pltpu.CompilerParams(vmem_limit_bytes=12 << 20),
        cost_estimate=cost(8 * row_block * depth * rank * width, 4 * row_block * depth * width),
        name="contract",
    )(placed_in(tensor, pltpu.HBM), placed_in(factor_c, pltpu.HBM))


def gram_terms(part_refs, rank):
    stacks = []
    for part in part_refs:
        value = part[:rank, :]
        first = value.astype(BF16)
        value = value - first.astype(F32)
        second = value.astype(BF16)
        third = (value - second.astype(F32)).astype(BF16)
        stacks.append(jnp.concatenate([first, second, third], axis=0))
    stack = jnp.concatenate(stacks, axis=1)
    terms = lax.dot_general(stack, stack, NT, preferred_element_type=F32)
    terms = terms[:, 2 * rank :] + terms[:, rank : 2 * rank] + terms[:, :rank]
    return terms[2 * rank :, :] + terms[rank : 2 * rank, :] + terms[:rank, :]


def weighted_sums(q_ref, part_refs, shifts):
    row_block, rank, _ = q_ref.shape
    width = part_refs[0].shape[1]
    here = lax.axis_index("ka")
    for tile in range(rank // SUBLANES):
        rows = pl.ds(tile * SUBLANES, SUBLANES)
        for i in range(row_block):
            total = None
            for s, part in zip(shifts, part_refs):
                start = (here ^ s) * width
                for c in range(0, width, LANES):
                    columns = pl.ds(pl.multiple_of(start + c, LANES), LANES)
                    term = q_ref[i, rows, columns] * part[rows, c : c + LANES]
                    total = term if total is None else total + term
            yield tile, i, total


def early_kernel(q_ref, *refs, shifts):
    part_refs, (sums_ref, gram_ref) = refs[:-2], refs[-2:]
    row_block, rank, _ = q_ref.shape
    gram_ref[...] = fold(gram_terms(part_refs, rank))
    for tile, i, total in weighted_sums(q_ref, part_refs, shifts):
        at = (tile * row_block + i) * SUBLANES
        sums_ref[at : at + SUBLANES, :] = total


def late_kernel(q_ref, sums_ref, gram_ref, *refs, shifts):
    part_refs, out_ref = refs[:-1], refs[-1]
    row_block, rank, _ = q_ref.shape
    half = rank // 2
    gram = fold(gram_terms(part_refs, rank))
    lane = lax.broadcasted_iota(jnp.int32, (SUBLANES, LANES), 1)
    groups = (out_ref.shape[0] - half) // SUBLANES
    packed = [jnp.zeros((SUBLANES, LANES), F32) for _ in range(groups)]
    for tile, i, total in weighted_sums(q_ref, part_refs, shifts):
        at = (tile * row_block + i) * SUBLANES
        total = total + sums_ref[at : at + SUBLANES, :]
        group, place = divmod(tile * row_block + i, LANES)
        packed[group] = jnp.where(
            lane == place, jnp.sum(total, axis=1, keepdims=True), packed[group]
        )
    for group, value in enumerate(packed):
        start = half + group * SUBLANES
        out_ref[start : start + SUBLANES, :] = value
    out_ref[:half, :] = gram + gram_ref[...]


def mode_one_sums(q, parts):
    row_block, rank, width = q.shape
    lines = row_block * rank // LANES
    count = len(parts)
    split = {0, count - 1}
    early = [s for s in range(count) if s in split]
    late = [s for s in reversed(range(count)) if s not in split]
    params = pltpu.CompilerParams(vmem_limit_bytes=6 << 20)
    work = cost(row_block * rank * width, 2 * row_block * rank * width)
    q = placed_in(q, pltpu.VMEM)
    sums, gram = pl.pallas_call(
        functools.partial(early_kernel, shifts=early),
        out_shape=(
            pltpu.VMEM((row_block * rank, LANES), F32),
            pltpu.VMEM((rank // 2, 2 * rank), F32),
        ),
        in_specs=[VMEM] * (1 + len(early)),
        out_specs=[VMEM] * 2,
        compiler_params=params,
        cost_estimate=work,
        name="mode_one_early",
    )(q, *[parts[s] for s in early])
    return pl.pallas_call(
        functools.partial(late_kernel, shifts=late),
        out_shape=pltpu.VMEM((rank // 2 + lines, LANES), F32),
        in_specs=[VMEM] * (3 + len(late)),
        out_specs=VMEM,
        compiler_params=params,
        cost_estimate=work,
        name="mode_one_late",
    )(q, sums, gram, *[parts[s] for s in late])


def gram_c_kernel(*refs):
    part_refs, out_ref = refs[:-1], refs[-1]
    rank = out_ref.shape[1] // 2
    rows = []
    for ref in part_refs:
        tail = ref[rank:, :]
        rows += [tail[:, g * rank : (g + 1) * rank] for g in range(tail.shape[1] // rank)]
    c = jnp.concatenate(rows, axis=0)
    out_ref[...] = fold(dot(c, c, TN))


def gram_of_c(parts, rank):
    return pl.pallas_call(
        gram_c_kernel,
        out_shape=pltpu.VMEM((rank // 2, 2 * rank), F32),
        in_specs=[VMEM] * len(parts),
        out_specs=VMEM,
        compiler_params=pltpu.CompilerParams(vmem_limit_bytes=4 << 20),
        cost_estimate=cost(10000000, 1000000),
        name="gram_c",
    )(*parts)


def add_kernel(*refs):
    part_refs, out_ref = refs[:-1], refs[-1]
    out_ref[...] = total_of(part_refs, part_refs[0].shape[0] - out_ref.shape[0])


def add_tail(parts, lines):
    return pl.pallas_call(
        add_kernel,
        out_shape=pltpu.VMEM((lines, LANES), F32),
        in_specs=[VMEM] * len(parts),
        out_specs=VMEM,
        compiler_params=pltpu.CompilerParams(vmem_limit_bytes=2 << 20),
        name="add_tail",
    )(*parts)


def solve_rows(pivot, rows):
    count = len(rows)
    rows = list(rows)
    block = {(q, s): pivot[q][s] for q in range(count) for s in range(q, count)}
    upper = {}
    for m in range(0, count, 2):
        a, b, d = block[m, m], block[m, m + 1], block[m + 1, m + 1]
        scale = 1.0 / (a * d - b * b)
        a, b, d = a * scale, b * scale, d * scale
        rows[m], rows[m + 1] = d * rows[m] - b * rows[m + 1], a * rows[m + 1] - b * rows[m]
        for s in range(m + 2, count):
            v, w = block[m, s], block[m + 1, s]
            upper[m, s], upper[m + 1, s] = d * v - b * w, a * w - b * v
        for q in range(m + 2, count):
            v, w = block[m, q], block[m + 1, q]
            for s in range(q, count):
                block[q, s] = block[q, s] - (v * upper[m, s] + w * upper[m + 1, s])
            rows[q] = rows[q] - (v * rows[m] + w * rows[m + 1])
    for m in range(count - 4, -1, -2):
        for s in range(m + 2, count):
            rows[m] = rows[m] - upper[m, s] * rows[s]
            rows[m + 1] = rows[m + 1] - upper[m + 1, s] * rows[s]
    return rows


def spd_inverse(matrix):
    n = matrix.shape[0]
    row = lax.broadcasted_iota(jnp.int32, (n, n), 0)
    column = lax.broadcasted_iota(jnp.int32, (n, n), 1)
    wide = jnp.concatenate([matrix, jnp.where(row == column, 1.0, 0.0).astype(F32)], axis=1)
    shape = (SUBLANES, 2 * n)
    tiles = [wide[t * SUBLANES : (t + 1) * SUBLANES, :] for t in range(n // SUBLANES)]
    sublane = lax.broadcasted_iota(jnp.int32, shape, 0)
    for k, block in enumerate(tiles):
        block = tiles[k]
        at = k * SUBLANES
        columns = [
            [jnp.broadcast_to(tile[:, at + q : at + q + 1], shape) for q in range(SUBLANES)]
            for tile in tiles
        ]
        rows = [jnp.broadcast_to(block[q : q + 1, :], shape) for q in range(SUBLANES)]
        pivot = [
            [jnp.broadcast_to(columns[k][s][q : q + 1, :], shape) for s in range(SUBLANES)]
            for q in range(SUBLANES)
        ]
        rows = solve_rows(pivot, rows)
        updated = []
        for t, tile in enumerate(tiles):
            if t == k:
                value = rows[0]
                for q in range(1, SUBLANES):
                    value = jnp.where(sublane == q, rows[q], value)
            else:
                value = tile
                for q in range(SUBLANES):
                    value = value - columns[t][q] * rows[q]
            updated.append(value)
        tiles = updated
    return jnp.concatenate([tile[:, n:] for tile in tiles], axis=0)


def inverse_kernel(*refs):
    gram_refs, (gram_c_ref, out_ref) = refs[:-2], refs[-2:]
    gram_b = total_of(gram_refs, 0, gram_c_ref.shape[0])
    out_ref[...] = spd_inverse(unfold(gram_b * gram_c_ref[...]))


def inverse(grams_b, gram_c):
    rank = gram_c.shape[1] // 2
    return pl.pallas_call(
        inverse_kernel,
        out_shape=jax.ShapeDtypeStruct((rank, rank), F32),
        in_specs=[VMEM] * (len(grams_b) + 1),
        out_specs=VMEM,
        compiler_params=pltpu.CompilerParams(vmem_limit_bytes=4 << 20),
        cost_estimate=cost(4000000, 4000000),
        name="inverse",
    )(*grams_b, gram_c)


def weigh(q_ref, factors, outs):
    row_block, rank, _ = q_ref.shape
    for tile in range(rank // SUBLANES):
        rows = pl.ds(tile * SUBLANES, SUBLANES)
        weights = [
            jnp.broadcast_to(
                factors[tile * SUBLANES : (tile + 1) * SUBLANES, i : i + 1], (SUBLANES, LANES)
            )
            for i in range(row_block)
        ]
        for out_ref, start, at, width in outs:
            for c in range(0, width, LANES):
                columns = pl.ds(pl.multiple_of(start + c, LANES), LANES)
                total = weights[0] * q_ref[0, rows, columns]
                for i in range(1, row_block):
                    total = total + weights[i] * q_ref[i, rows, columns]
                out_ref[rows, at + c : at + c + LANES] = total


def targets(q_ref, out_ref, shifts, other):
    side = lax.axis_index("ia") % 2
    side = 1 - side if other else side
    half = q_ref.shape[2] // 2
    width = half // lax.axis_size("ka")
    here = lax.axis_index("ka")
    return [
        (out_ref, side * half + (here ^ s) * width, n * width, width)
        for n, s in enumerate(shifts)
    ]


def solve_kernel(q_ref, inv_ref, *refs, shifts):
    sum_refs, (a_ref, factors_ref, send_ref) = refs[:-3], refs[-3:]
    row_block, rank, _ = q_ref.shape
    packed = total_of(sum_refs)
    columns = []
    for tile in range(rank // SUBLANES):
        group, place = divmod(tile * row_block, LANES)
        columns.append(
            packed[group * SUBLANES : (group + 1) * SUBLANES, place : place + row_block]
        )
    factors = dot(inv_ref[...], jnp.concatenate(columns, axis=0), NN)
    factors_ref[...] = factors
    weigh(q_ref, factors, targets(q_ref, send_ref, shifts, True))
    mine = lax.axis_index("ja") * lax.axis_size("ka") + lax.axis_index("ka")
    lane = lax.broadcasted_iota(jnp.int32, (rank, row_block), 1)
    chosen = jnp.where(lane == mine, factors, 0.0)
    a_ref[...] = dot(jnp.ones((SUBLANES, row_block), F32), chosen, NT)[:1, :]


def weigh_kernel(q_ref, factors_ref, out_ref, *, shifts, other):
    weigh(q_ref, factors_ref[...], targets(q_ref, out_ref, shifts, other))


def share(q, shifts):
    row_block, rank, width = q.shape
    columns = width // 2 // lax.axis_size("ka") * len(shifts)
    return (
        pltpu.VMEM((rank, columns), F32),
        cost(2 * row_block * rank * columns, 4 * row_block * rank * columns),
    )


def solve_and_weigh(q, inv, sums, shifts):
    row_block, rank, _ = q.shape
    shape, work = share(q, shifts)
    return pl.pallas_call(
        functools.partial(solve_kernel, shifts=shifts),
        out_shape=(
            jax.ShapeDtypeStruct((1, rank), F32),
            pltpu.VMEM((rank, row_block), F32),
            shape,
        ),
        in_specs=[VMEM] * (2 + len(sums)),
        out_specs=[VMEM] * 3,
        compiler_params=pltpu.CompilerParams(vmem_limit_bytes=4 << 20),
        cost_estimate=work,
        name="solve",
    )(placed_in(q, pltpu.VMEM), inv, *sums)


def weigh_columns(q, factors, shifts, other):
    shape, work = share(q, shifts)
    return pl.pallas_call(
        functools.partial(weigh_kernel, shifts=shifts, other=other),
        out_shape=shape,
        in_specs=[VMEM] * 2,
        out_specs=VMEM,
        compiler_params=pltpu.CompilerParams(vmem_limit_bytes=4 << 20),
        cost_estimate=work,
        name="weigh",
    )(placed_in(q, pltpu.VMEM), factors)


def split_kernel(kept_ref, got_ref, *out_refs):
    width = out_refs[0].shape[1]
    for n, out_ref in enumerate(out_refs):
        columns = pl.ds(n * width, width)
        out_ref[...] = kept_ref[:, columns] + got_ref[:, columns]


def split_sums(kept, got, count):
    rank, columns = kept.shape
    return pl.pallas_call(
        split_kernel,
        out_shape=[pltpu.VMEM((rank, columns // count), F32)] * count,
        in_specs=[VMEM] * 2,
        out_specs=[VMEM] * count,
        compiler_params=pltpu.CompilerParams(vmem_limit_bytes=2 << 20),
        name="split_sums",
    )(kept, got)


def final_kernel(*refs):
    part_refs, out_ref = refs[:-1], refs[-1]
    out_ref[:, 0, :] = total_of(part_refs)


def final_sum(parts):
    rank, width = parts[0].shape
    return pl.pallas_call(
        final_kernel,
        out_shape=jax.ShapeDtypeStruct((rank, 1, width), F32),
        in_specs=[VMEM] * len(parts),
        out_specs=VMEM,
        compiler_params=pltpu.CompilerParams(vmem_limit_bytes=2 << 20),
        name="final_sum",
    )(*parts)


def swap(x, axis, s):
    n = lax.axis_size(axis)
    return lax.ppermute(x, axis, [(i, i ^ s) for i in range(n)])


def swaps(x, axis):
    n = lax.axis_size(axis)
    got = {s: swap(x, axis, s) for s in reversed(range(1, n))}
    return [x] + [got[s] for s in range(1, n)]


def body(tensor, factor_b, factor_c):
    row_block, depth, width = tensor.shape
    rank = factor_c.shape[1]
    n_ia, n_ka = lax.axis_size("ia"), lax.axis_size("ka")
    lines = row_block * rank // LANES
    parts = swaps(pack(factor_b.T, factor_c), "ka")
    q = contract(tensor, factor_c)
    sums = swaps(mode_one_sums(q, parts), "ja")
    gram_c = gram_of_c(parts, rank)
    tails = swaps(add_tail(sums, lines), "ka")
    inv = inverse(sums, gram_c)
    far = list(reversed(range(2, n_ka)))
    near = [1, 0]
    if n_ia == 2 and width % (n_ia * n_ka * LANES) == 0:
        a_row, factors, send = solve_and_weigh(q, inv, tails, far)
        got = swap(send, "ia", 1)
        send_near = weigh_columns(q, factors, near, True)
        got_near = swap(send_near, "ia", 1)
        kept = weigh_columns(q, factors, far, False)
        kept_near = weigh_columns(q, factors, near, False)
        pieces = split_sums(kept, got, len(far))
        final = [swap(piece, "ka", s) for piece, s in zip(pieces, far)]
        next_piece, own = split_sums(kept_near, got_near, len(near))
        return a_row, final_sum([own, swap(next_piece, "ka", 1)] + final[::-1])
    a_row, factors, _ = solve_and_weigh(q, inv, tails, near)
    whole = jnp.einsum("irj,ri->rj", q, factors, precision=HIGHEST)
    reduced = lax.psum_scatter(whole, ("ia", "ka"), scatter_dimension=1, tiled=True)
    return a_row, reduced.reshape(rank, 1, reduced.shape[1])


def solution(mesh):
    placed = (P("ia", "ka", "ja"), P(("ja", "ka"), None), P("ka", None))
    return jax.shard_map(
        body,
        mesh=mesh,
        in_specs=placed,
        out_specs=(P(("ia", "ja", "ka"), None), P(None, "ja", ("ia", "ka"))),
        check_vma=False,
    )
```

```python
import functools

import jax
import jax.numpy as jnp
from jax import lax
from jax.experimental import pallas as pl
from jax.experimental.pallas import tpu as pltpu
from jax.sharding import PartitionSpec as P


F32 = jnp.float32
BF16 = jnp.bfloat16
HIGHEST = lax.Precision.HIGHEST
LANES = 128
SUBLANES = 8
VMEM = pl.BlockSpec(memory_space=pltpu.VMEM)
HBM = pl.BlockSpec(memory_space=pltpu.HBM)
NN = (((1,), (0,)), ((), ()))
NT = (((1,), (1,)), ((), ()))
TN = (((0,), (0,)), ((), ()))


def dot(a, b, dims):
    return lax.dot_general(a, b, dims, precision=HIGHEST, preferred_element_type=F32)


def cost(flops, bytes_accessed):
    return pl.CostEstimate(flops=flops, bytes_accessed=bytes_accessed, transcendentals=0)


def placed_in(x, space):
    return pltpu.with_memory_space_constraint(x, space)


def fold(square):
    half = square.shape[0] // 2
    return jnp.concatenate([square[:half, :], square[half:, :]], axis=1)


def unfold(folded):
    half = folded.shape[1] // 2
    return jnp.concatenate([folded[:, :half], folded[:, half:]], axis=0)


def total_of(refs, start=0, stop=None):
    total = refs[0][start:stop, :]
    for ref in refs[1:]:
        total = total + ref[start:stop, :]
    return total


def contract_kernel(
    x_hbm, c_hbm, q_ref, gram_ref, x_ref, c_ref, lhs_ref, x_sems, c_sem, *, chunks
):
    rows = q_ref.shape[0] // chunks
    copies = [
        pltpu.make_async_copy(
            x_hbm.at[pl.ds(n * rows, rows)], x_ref.at[pl.ds(n * rows, rows)], x_sems.at[n]
        )
        for n in range(chunks)
    ]
    c_copy = pltpu.make_async_copy(c_hbm, c_ref, c_sem)
    c_copy.start()
    for copy in copies:
        copy.start()
    c_copy.wait()
    c = c_ref[...]
    gram_ref[...] = fold(dot(c, c, TN))
    ct = c.T
    high = ct.astype(BF16)
    low = (ct - high.astype(F32)).astype(BF16)
    lhs_ref[...] = jnp.concatenate([high, low, high, low], axis=1)
    for n, copy in enumerate(copies):
        copy.wait()
        for i in range(n * rows, (n + 1) * rows):
            x = x_ref[i]
            high = x.astype(BF16)
            low = (x - high.astype(F32)).astype(BF16)
            rhs = jnp.concatenate([high, high, low, low], axis=0)
            q_ref[i] = jnp.dot(lhs_ref[...], rhs, preferred_element_type=F32)


def contract(tensor, factor_c):
    row_block, depth, width = tensor.shape
    rank = factor_c.shape[1]
    chunks = 4
    return pl.pallas_call(
        functools.partial(contract_kernel, chunks=chunks),
        out_shape=(
            pltpu.VMEM((row_block, rank, width), F32),
            pltpu.VMEM((rank // 2, 2 * rank), F32),
        ),
        in_specs=[HBM, HBM],
        out_specs=[VMEM, VMEM],
        scratch_shapes=[
            pltpu.VMEM(tensor.shape, F32),
            pltpu.VMEM(factor_c.shape, F32),
            pltpu.VMEM((rank, 4 * depth), BF16),
            pltpu.SemaphoreType.DMA((chunks,)),
            pltpu.SemaphoreType.DMA,
        ],
        compiler_params=pltpu.CompilerParams(vmem_limit_bytes=12 << 20),
        cost_estimate=cost(8 * row_block * depth * rank * width, 4 * row_block * depth * width),
        name="contract",
    )(placed_in(tensor, pltpu.HBM), placed_in(factor_c, pltpu.HBM))


def gram_terms(part_refs, rank):
    stacks = []
    for part in part_refs:
        value = part[:rank, :]
        first = value.astype(BF16)
        value = value - first.astype(F32)
        second = value.astype(BF16)
        third = (value - second.astype(F32)).astype(BF16)
        stacks.append(jnp.concatenate([first, second, third], axis=0))
    stack = jnp.concatenate(stacks, axis=1)
    terms = lax.dot_general(stack, stack, NT, preferred_element_type=F32)
    terms = terms[:, 2 * rank :] + terms[:, rank : 2 * rank] + terms[:, :rank]
    return terms[2 * rank :, :] + terms[rank : 2 * rank, :] + terms[:rank, :]


def weighted_sums(q_ref, part_refs, shifts):
    row_block, rank, _ = q_ref.shape
    width = part_refs[0].shape[1]
    here = lax.axis_index("ka")
    for tile in range(rank // SUBLANES):
        rows = pl.ds(tile * SUBLANES, SUBLANES)
        for i in range(row_block):
            total = None
            for s, part in zip(shifts, part_refs):
                start = (here ^ s) * width
                for c in range(0, width, LANES):
                    columns = pl.ds(pl.multiple_of(start + c, LANES), LANES)
                    term = q_ref[i, rows, columns] * part[rows, c : c + LANES]
                    total = term if total is None else total + term
            yield tile, i, total


def early_kernel(q_ref, *refs, shifts):
    part_refs, (sums_ref, gram_ref) = refs[:-2], refs[-2:]
    row_block, rank, _ = q_ref.shape
    gram_ref[...] = fold(gram_terms(part_refs, rank))
    for tile, i, total in weighted_sums(q_ref, part_refs, shifts):
        at = (tile * row_block + i) * SUBLANES
        sums_ref[at : at + SUBLANES, :] = total


def late_kernel(q_ref, sums_ref, gram_ref, *refs, shifts):
    part_refs, out_ref = refs[:-1], refs[-1]
    row_block, rank, _ = q_ref.shape
    half = rank // 2
    gram = fold(gram_terms(part_refs, rank))
    lane = lax.broadcasted_iota(jnp.int32, (SUBLANES, LANES), 1)
    groups = (out_ref.shape[0] - half) // SUBLANES
    packed = [jnp.zeros((SUBLANES, LANES), F32) for _ in range(groups)]
    for tile, i, total in weighted_sums(q_ref, part_refs, shifts):
        at = (tile * row_block + i) * SUBLANES
        total = total + sums_ref[at : at + SUBLANES, :]
        group, place = divmod(tile * row_block + i, LANES)
        packed[group] = jnp.where(
            lane == place, jnp.sum(total, axis=1, keepdims=True), packed[group]
        )
    for group, value in enumerate(packed):
        start = half + group * SUBLANES
        out_ref[start : start + SUBLANES, :] = value
    out_ref[:half, :] = gram + gram_ref[...]


def mode_one_sums(q, parts):
    row_block, rank, width = q.shape
    lines = row_block * rank // LANES
    count = len(parts)
    split = {0, count - 1}
    early = [s for s in range(count) if s in split]
    late = [s for s in reversed(range(count)) if s not in split]
    params = pltpu.CompilerParams(vmem_limit_bytes=6 << 20)
    work = cost(row_block * rank * width, 2 * row_block * rank * width)
    q = placed_in(q, pltpu.VMEM)
    sums, gram = pl.pallas_call(
        functools.partial(early_kernel, shifts=early),
        out_shape=(
            pltpu.VMEM((row_block * rank, LANES), F32),
            pltpu.VMEM((rank // 2, 2 * rank), F32),
        ),
        in_specs=[VMEM] * (1 + len(early)),
        out_specs=[VMEM] * 2,
        compiler_params=params,
        cost_estimate=work,
        name="mode_one_early",
    )(q, *[parts[s] for s in early])
    return pl.pallas_call(
        functools.partial(late_kernel, shifts=late),
        out_shape=pltpu.VMEM((rank // 2 + lines, LANES), F32),
        in_specs=[VMEM] * (3 + len(late)),
        out_specs=VMEM,
        compiler_params=params,
        cost_estimate=work,
        name="mode_one_late",
    )(q, sums, gram, *[parts[s] for s in late])


def add_kernel(*refs):
    part_refs, out_ref = refs[:-1], refs[-1]
    out_ref[...] = total_of(part_refs, part_refs[0].shape[0] - out_ref.shape[0])


def add_tail(parts, lines):
    return pl.pallas_call(
        add_kernel,
        out_shape=pltpu.VMEM((lines, LANES), F32),
        in_specs=[VMEM] * len(parts),
        out_specs=VMEM,
        compiler_params=pltpu.CompilerParams(vmem_limit_bytes=2 << 20),
        name="add_tail",
    )(*parts)


def solve_rows(pivot, rows):
    count = len(rows)
    rows = list(rows)
    block = {(q, s): pivot[q][s] for q in range(count) for s in range(q, count)}
    upper = {}
    for m in range(0, count, 2):
        a, b, d = block[m, m], block[m, m + 1], block[m + 1, m + 1]
        scale = 1.0 / (a * d - b * b)
        a, b, d = a * scale, b * scale, d * scale
        rows[m], rows[m + 1] = d * rows[m] - b * rows[m + 1], a * rows[m + 1] - b * rows[m]
        for s in range(m + 2, count):
            v, w = block[m, s], block[m + 1, s]
            upper[m, s], upper[m + 1, s] = d * v - b * w, a * w - b * v
        for q in range(m + 2, count):
            v, w = block[m, q], block[m + 1, q]
            for s in range(q, count):
                block[q, s] = block[q, s] - (v * upper[m, s] + w * upper[m + 1, s])
            rows[q] = rows[q] - (v * rows[m] + w * rows[m + 1])
    for m in range(count - 4, -1, -2):
        for s in range(m + 2, count):
            rows[m] = rows[m] - upper[m, s] * rows[s]
            rows[m + 1] = rows[m + 1] - upper[m + 1, s] * rows[s]
    return rows


def spd_inverse(matrix):
    n = matrix.shape[0]
    row = lax.broadcasted_iota(jnp.int32, (n, n), 0)
    column = lax.broadcasted_iota(jnp.int32, (n, n), 1)
    wide = jnp.concatenate([matrix, jnp.where(row == column, 1.0, 0.0).astype(F32)], axis=1)
    shape = (SUBLANES, 2 * n)
    tiles = [wide[t * SUBLANES : (t + 1) * SUBLANES, :] for t in range(n // SUBLANES)]
    sublane = lax.broadcasted_iota(jnp.int32, shape, 0)
    for k, block in enumerate(tiles):
        block = tiles[k]
        at = k * SUBLANES
        columns = [
            [jnp.broadcast_to(tile[:, at + q : at + q + 1], shape) for q in range(SUBLANES)]
            for tile in tiles
        ]
        rows = [jnp.broadcast_to(block[q : q + 1, :], shape) for q in range(SUBLANES)]
        pivot = [
            [jnp.broadcast_to(columns[k][s][q : q + 1, :], shape) for s in range(SUBLANES)]
            for q in range(SUBLANES)
        ]
        rows = solve_rows(pivot, rows)
        updated = []
        for t, tile in enumerate(tiles):
            if t == k:
                value = rows[0]
                for q in range(1, SUBLANES):
                    value = jnp.where(sublane == q, rows[q], value)
            else:
                value = tile
                for q in range(SUBLANES):
                    value = value - columns[t][q] * rows[q]
            updated.append(value)
        tiles = updated
    return jnp.concatenate([tile[:, n:] for tile in tiles], axis=0)


def inverse_kernel(*refs):
    count = (len(refs) - 1) // 2
    gram_refs, c_refs, out_ref = refs[:count], refs[count:-1], refs[-1]
    gram_c = total_of(c_refs)
    gram_b = total_of(gram_refs, 0, gram_c.shape[0])
    out_ref[...] = spd_inverse(unfold(gram_b * gram_c))


def inverse(grams_b, grams_c):
    rank = grams_c[0].shape[1] // 2
    return pl.pallas_call(
        inverse_kernel,
        out_shape=pltpu.VMEM((rank, rank), F32),
        in_specs=[VMEM] * (len(grams_b) + len(grams_c)),
        out_specs=VMEM,
        compiler_params=pltpu.CompilerParams(vmem_limit_bytes=4 << 20),
        cost_estimate=cost(4000000, 4000000),
        name="inverse",
    )(*grams_b, *grams_c)


def weigh(q_ref, factors, outs):
    row_block, rank, _ = q_ref.shape
    for tile in range(rank // SUBLANES):
        rows = pl.ds(tile * SUBLANES, SUBLANES)
        weights = [
            jnp.broadcast_to(
                factors[tile * SUBLANES : (tile + 1) * SUBLANES, i : i + 1], (SUBLANES, LANES)
            )
            for i in range(row_block)
        ]
        for out_ref, start, at, width in outs:
            for c in range(0, width, LANES):
                columns = pl.ds(pl.multiple_of(start + c, LANES), LANES)
                total = weights[0] * q_ref[0, rows, columns]
                for i in range(1, row_block):
                    total = total + weights[i] * q_ref[i, rows, columns]
                out_ref[rows, at + c : at + c + LANES] = total


def targets(q_ref, out_ref, shifts, other):
    side = lax.axis_index("ia") % 2
    side = 1 - side if other else side
    half = q_ref.shape[2] // 2
    width = half // lax.axis_size("ka")
    here = lax.axis_index("ka")
    return [
        (out_ref, side * half + (here ^ s) * width, n * width, width)
        for n, s in enumerate(shifts)
    ]


def solve_kernel(q_ref, inv_ref, *refs, shifts):
    sum_refs, (a_ref, factors_ref, send_ref) = refs[:-3], refs[-3:]
    row_block, rank, _ = q_ref.shape
    packed = total_of(sum_refs)
    columns = []
    for tile in range(rank // SUBLANES):
        group, place = divmod(tile * row_block, LANES)
        columns.append(
            packed[group * SUBLANES : (group + 1) * SUBLANES, place : place + row_block]
        )
    factors = dot(inv_ref[...], jnp.concatenate(columns, axis=0), NN)
    factors_ref[...] = factors
    weigh(q_ref, factors, targets(q_ref, send_ref, shifts, True))
    mine = lax.axis_index("ja") * lax.axis_size("ka") + lax.axis_index("ka")
    lane = lax.broadcasted_iota(jnp.int32, (rank, row_block), 1)
    chosen = jnp.where(lane == mine, factors, 0.0)
    a_ref[...] = dot(jnp.ones((SUBLANES, row_block), F32), chosen, NT)[:1, :]


def weigh_kernel(q_ref, factors_ref, out_ref, *, shifts, other):
    weigh(q_ref, factors_ref[...], targets(q_ref, out_ref, shifts, other))


def share(q, shifts):
    row_block, rank, width = q.shape
    columns = width // 2 // lax.axis_size("ka") * len(shifts)
    return (
        pltpu.VMEM((rank, columns), F32),
        cost(2 * row_block * rank * columns, 4 * row_block * rank * columns),
    )


def solve_and_weigh(q, inv, sums, shifts):
    row_block, rank, _ = q.shape
    shape, work = share(q, shifts)
    return pl.pallas_call(
        functools.partial(solve_kernel, shifts=shifts),
        out_shape=(
            jax.ShapeDtypeStruct((1, rank), F32),
            pltpu.VMEM((rank, row_block), F32),
            shape,
        ),
        in_specs=[VMEM] * (2 + len(sums)),
        out_specs=[VMEM] * 3,
        compiler_params=pltpu.CompilerParams(vmem_limit_bytes=4 << 20),
        cost_estimate=work,
        name="solve",
    )(placed_in(q, pltpu.VMEM), inv, *sums)


def weigh_columns(q, factors, shifts, other):
    shape, work = share(q, shifts)
    return pl.pallas_call(
        functools.partial(weigh_kernel, shifts=shifts, other=other),
        out_shape=shape,
        in_specs=[VMEM] * 2,
        out_specs=VMEM,
        compiler_params=pltpu.CompilerParams(vmem_limit_bytes=4 << 20),
        cost_estimate=work,
        name="weigh",
    )(placed_in(q, pltpu.VMEM), factors)


def split_kernel(kept_ref, got_ref, *out_refs):
    width = out_refs[0].shape[1]
    for n, out_ref in enumerate(out_refs):
        columns = pl.ds(n * width, width)
        out_ref[...] = kept_ref[:, columns] + got_ref[:, columns]


def split_sums(kept, got, count):
    rank, columns = kept.shape
    return pl.pallas_call(
        split_kernel,
        out_shape=[pltpu.VMEM((rank, columns // count), F32)] * count,
        in_specs=[VMEM] * 2,
        out_specs=[VMEM] * count,
        compiler_params=pltpu.CompilerParams(vmem_limit_bytes=2 << 20),
        name="split_sums",
    )(kept, got)


def final_kernel(*refs):
    part_refs, out_ref = refs[:-1], refs[-1]
    out_ref[:, 0, :] = total_of(part_refs)


def final_sum(parts):
    rank, width = parts[0].shape
    return pl.pallas_call(
        final_kernel,
        out_shape=jax.ShapeDtypeStruct((rank, 1, width), F32),
        in_specs=[VMEM] * len(parts),
        out_specs=VMEM,
        compiler_params=pltpu.CompilerParams(vmem_limit_bytes=2 << 20),
        name="final_sum",
    )(*parts)


def swap(x, axis, s):
    n = lax.axis_size(axis)
    return lax.ppermute(x, axis, [(i, i ^ s) for i in range(n)])


def swaps(x, axis):
    n = lax.axis_size(axis)
    return [x] + [swap(x, axis, s) for s in range(1, n)]


def body(tensor, factor_b, factor_c):
    row_block, _, width = tensor.shape
    rank = factor_c.shape[1]
    n_ia, n_ka = lax.axis_size("ia"), lax.axis_size("ka")
    lines = row_block * rank // LANES
    parts = swaps(factor_b.T, "ka")
    q, gram_c = contract(tensor, factor_c)
    grams_c = swaps(gram_c, "ka")
    sums = swaps(mode_one_sums(q, parts), "ja")
    tails = swaps(add_tail(sums, lines), "ka")
    inv = inverse(sums, grams_c)
    far = list(reversed(range(2, n_ka)))
    near = [1, 0]
    if n_ia == 2 and width % (n_ia * n_ka * LANES) == 0:
        a_row, factors, send = solve_and_weigh(q, inv, tails, far)
        got = swap(send, "ia", 1)
        send_near = weigh_columns(q, factors, near, True)
        got_near = swap(send_near, "ia", 1)
        kept = weigh_columns(q, factors, far, False)
        kept_near = weigh_columns(q, factors, near, False)
        pieces = split_sums(kept, got, len(far))
        final = [swap(piece, "ka", s) for piece, s in zip(pieces, far)]
        next_piece, own = split_sums(kept_near, got_near, len(near))
        final.append(swap(next_piece, "ka", 1))
        return a_row, final_sum([own] + final[::-1])
    a_row, factors, _ = solve_and_weigh(q, inv, tails, near)
    whole = jnp.einsum("irj,ri->rj", q, factors, precision=HIGHEST)
    reduced = lax.psum_scatter(whole, ("ia", "ka"), scatter_dimension=1, tiled=True)
    return a_row, reduced.reshape(rank, 1, reduced.shape[1])


def solution(mesh):
    placed = (P("ia", "ka", "ja"), P(("ja", "ka"), None), P("ka", None))
    return jax.shard_map(
        body,
        mesh=mesh,
        in_specs=placed,
        out_specs=(P(("ia", "ja", "ka"), None), P(None, "ja", ("ia", "ka"))),
        check_vma=False,
    )
```

```python
import functools

import jax
import jax.numpy as jnp
from jax import lax
from jax.experimental import pallas as pl
from jax.experimental.pallas import tpu as pltpu
from jax.sharding import PartitionSpec as P


F32 = jnp.float32
BF16 = jnp.bfloat16
HIGHEST = lax.Precision.HIGHEST
LANES = 128
SUBLANES = 8
VMEM = pl.BlockSpec(memory_space=pltpu.VMEM)
HBM = pl.BlockSpec(memory_space=pltpu.HBM)
NN = (((1,), (0,)), ((), ()))
NT = (((1,), (1,)), ((), ()))
TN = (((0,), (0,)), ((), ()))


def dot(a, b, dims):
    return lax.dot_general(a, b, dims, precision=HIGHEST, preferred_element_type=F32)


def cost(flops, bytes_accessed):
    return pl.CostEstimate(flops=flops, bytes_accessed=bytes_accessed, transcendentals=0)


def placed_in(x, space):
    return pltpu.with_memory_space_constraint(x, space)


def fold(square):
    half = square.shape[0] // 2
    return jnp.concatenate([square[:half, :], square[half:, :]], axis=1)


def unfold(folded):
    half = folded.shape[1] // 2
    return jnp.concatenate([folded[:, :half], folded[:, half:]], axis=0)


def total_of(refs, start=0, stop=None):
    total = refs[0][start:stop, :]
    for ref in refs[1:]:
        total = total + ref[start:stop, :]
    return total


def contract_kernel(
    x_hbm, b_hbm, c_hbm, q_ref, gram_b_ref, gram_c_ref, x_ref, b_ref, c_ref, lhs_ref, sems, *, chunks
):
    rows = q_ref.shape[0] // chunks
    copies = [
        pltpu.make_async_copy(
            x_hbm.at[pl.ds(n * rows, rows)], x_ref.at[pl.ds(n * rows, rows)], sems.at[n]
        )
        for n in range(chunks)
    ]
    c_copy = pltpu.make_async_copy(c_hbm, c_ref, sems.at[chunks])
    b_copy = pltpu.make_async_copy(b_hbm, b_ref, sems.at[chunks + 1])
    c_copy.start()
    b_copy.start()
    for copy in copies:
        copy.start()
    c_copy.wait()
    b_copy.wait()
    c = c_ref[...]
    gram_c_ref[...] = fold(dot(c, c, TN))
    gram_b_ref[...] = fold(gram_terms([b_ref], b_ref.shape[0]))
    ct = c.T
    high = ct.astype(BF16)
    low = (ct - high.astype(F32)).astype(BF16)
    lhs_ref[...] = jnp.concatenate([high, low, high, low], axis=1)
    for n, copy in enumerate(copies):
        copy.wait()
        for i in range(n * rows, (n + 1) * rows):
            x = x_ref[i]
            high = x.astype(BF16)
            low = (x - high.astype(F32)).astype(BF16)
            rhs = jnp.concatenate([high, high, low, low], axis=0)
            q_ref[i] = jnp.dot(lhs_ref[...], rhs, preferred_element_type=F32)


def contract(tensor, bt, factor_c):
    row_block, depth, width = tensor.shape
    rank = factor_c.shape[1]
    chunks = 4
    return pl.pallas_call(
        functools.partial(contract_kernel, chunks=chunks),
        out_shape=(
            pltpu.VMEM((row_block, rank, width), F32),
            pltpu.VMEM((rank // 2, 2 * rank), F32),
            pltpu.VMEM((rank // 2, 2 * rank), F32),
        ),
        in_specs=[HBM] * 3,
        out_specs=[VMEM] * 3,
        scratch_shapes=[
            pltpu.VMEM(tensor.shape, F32),
            pltpu.VMEM(bt.shape, F32),
            pltpu.VMEM(factor_c.shape, F32),
            pltpu.VMEM((rank, 4 * depth), BF16),
            pltpu.SemaphoreType.DMA((chunks + 2,)),
        ],
        compiler_params=pltpu.CompilerParams(vmem_limit_bytes=12 << 20),
        cost_estimate=cost(8 * row_block * depth * rank * width, 4 * row_block * depth * width),
        name="contract",
    )(*(placed_in(x, pltpu.HBM) for x in (tensor, bt, factor_c)))


def gram_terms(part_refs, rank):
    stacks = []
    for part in part_refs:
        value = part[:rank, :]
        first = value.astype(BF16)
        value = value - first.astype(F32)
        second = value.astype(BF16)
        third = (value - second.astype(F32)).astype(BF16)
        stacks.append(jnp.concatenate([first, second, third], axis=0))
    stack = jnp.concatenate(stacks, axis=1)
    terms = lax.dot_general(stack, stack, NT, preferred_element_type=F32)
    terms = terms[:, 2 * rank :] + terms[:, rank : 2 * rank] + terms[:, :rank]
    return terms[2 * rank :, :] + terms[rank : 2 * rank, :] + terms[:rank, :]


def weighted_sums(q_ref, part_refs, shifts):
    row_block, rank, _ = q_ref.shape
    width = part_refs[0].shape[1]
    here = lax.axis_index("ka")
    for tile in range(rank // SUBLANES):
        rows = pl.ds(tile * SUBLANES, SUBLANES)
        for i in range(row_block):
            total = None
            for s, part in zip(shifts, part_refs):
                start = (here ^ s) * width
                for c in range(0, width, LANES):
                    columns = pl.ds(pl.multiple_of(start + c, LANES), LANES)
                    term = q_ref[i, rows, columns] * part[rows, c : c + LANES]
                    total = term if total is None else total + term
            yield tile, i, total


def early_kernel(q_ref, own_ref, *refs, shifts):
    part_refs, (sums_ref, gram_ref) = refs[:-2], refs[-2:]
    row_block, rank, _ = q_ref.shape
    others = [part for s, part in zip(shifts, part_refs) if s != 0]
    gram_ref[...] = fold(gram_terms(others, rank)) + own_ref[...]
    for tile, i, total in weighted_sums(q_ref, part_refs, shifts):
        at = (tile * row_block + i) * SUBLANES
        sums_ref[at : at + SUBLANES, :] = total


def late_kernel(q_ref, sums_ref, gram_ref, *refs, shifts):
    part_refs, out_ref = refs[:-1], refs[-1]
    row_block, rank, _ = q_ref.shape
    half = rank // 2
    gram = fold(gram_terms(part_refs, rank))
    lane = lax.broadcasted_iota(jnp.int32, (SUBLANES, LANES), 1)
    groups = (out_ref.shape[0] - half) // SUBLANES
    packed = [jnp.zeros((SUBLANES, LANES), F32) for _ in range(groups)]
    for tile, i, total in weighted_sums(q_ref, part_refs, shifts):
        at = (tile * row_block + i) * SUBLANES
        total = total + sums_ref[at : at + SUBLANES, :]
        group, place = divmod(tile * row_block + i, LANES)
        packed[group] = jnp.where(
            lane == place, jnp.sum(total, axis=1, keepdims=True), packed[group]
        )
    for group, value in enumerate(packed):
        start = half + group * SUBLANES
        out_ref[start : start + SUBLANES, :] = value
    out_ref[:half, :] = gram + gram_ref[...]


def mode_one_sums(q, own_gram, parts):
    row_block, rank, width = q.shape
    lines = row_block * rank // LANES
    count = len(parts)
    split = {0, count - 1}
    early = [s for s in range(count) if s in split]
    late = [s for s in reversed(range(count)) if s not in split]
    params = pltpu.CompilerParams(vmem_limit_bytes=6 << 20)
    work = cost(row_block * rank * width, 2 * row_block * rank * width)
    q = placed_in(q, pltpu.VMEM)
    sums, gram = pl.pallas_call(
        functools.partial(early_kernel, shifts=early),
        out_shape=(
            pltpu.VMEM((row_block * rank, LANES), F32),
            pltpu.VMEM((rank // 2, 2 * rank), F32),
        ),
        in_specs=[VMEM] * (2 + len(early)),
        out_specs=[VMEM] * 2,
        compiler_params=params,
        cost_estimate=work,
        name="mode_one_early",
    )(q, own_gram, *[parts[s] for s in early])
    return pl.pallas_call(
        functools.partial(late_kernel, shifts=late),
        out_shape=pltpu.VMEM((rank // 2 + lines, LANES), F32),
        in_specs=[VMEM] * (3 + len(late)),
        out_specs=VMEM,
        compiler_params=params,
        cost_estimate=work,
        name="mode_one_late",
    )(q, sums, gram, *[parts[s] for s in late])


def add_kernel(*refs):
    part_refs, out_ref = refs[:-1], refs[-1]
    out_ref[...] = total_of(part_refs, part_refs[0].shape[0] - out_ref.shape[0])


def add_tail(parts, lines):
    return pl.pallas_call(
        add_kernel,
        out_shape=pltpu.VMEM((lines, LANES), F32),
        in_specs=[VMEM] * len(parts),
        out_specs=VMEM,
        compiler_params=pltpu.CompilerParams(vmem_limit_bytes=2 << 20),
        name="add_tail",
    )(*parts)


def solve_rows(pivot, rows):
    count = len(rows)
    rows = list(rows)
    block = {(q, s): pivot[q][s] for q in range(count) for s in range(q, count)}
    upper = {}
    for m in range(0, count, 2):
        a, b, d = block[m, m], block[m, m + 1], block[m + 1, m + 1]
        scale = 1.0 / (a * d - b * b)
        a, b, d = a * scale, b * scale, d * scale
        rows[m], rows[m + 1] = d * rows[m] - b * rows[m + 1], a * rows[m + 1] - b * rows[m]
        for s in range(m + 2, count):
            v, w = block[m, s], block[m + 1, s]
            upper[m, s], upper[m + 1, s] = d * v - b * w, a * w - b * v
        for q in range(m + 2, count):
            v, w = block[m, q], block[m + 1, q]
            for s in range(q, count):
                block[q, s] = block[q, s] - (v * upper[m, s] + w * upper[m + 1, s])
            rows[q] = rows[q] - (v * rows[m] + w * rows[m + 1])
    for m in range(count - 4, -1, -2):
        for s in range(m + 2, count):
            rows[m] = rows[m] - upper[m, s] * rows[s]
            rows[m + 1] = rows[m + 1] - upper[m + 1, s] * rows[s]
    return rows


def spd_inverse(matrix):
    n = matrix.shape[0]
    row = lax.broadcasted_iota(jnp.int32, (n, n), 0)
    column = lax.broadcasted_iota(jnp.int32, (n, n), 1)
    wide = jnp.concatenate([matrix, jnp.where(row == column, 1.0, 0.0).astype(F32)], axis=1)
    shape = (SUBLANES, 2 * n)
    tiles = [wide[t * SUBLANES : (t + 1) * SUBLANES, :] for t in range(n // SUBLANES)]
    sublane = lax.broadcasted_iota(jnp.int32, shape, 0)
    for k, block in enumerate(tiles):
        block = tiles[k]
        at = k * SUBLANES
        columns = [
            [jnp.broadcast_to(tile[:, at + q : at + q + 1], shape) for q in range(SUBLANES)]
            for tile in tiles
        ]
        rows = [jnp.broadcast_to(block[q : q + 1, :], shape) for q in range(SUBLANES)]
        pivot = [
            [jnp.broadcast_to(columns[k][s][q : q + 1, :], shape) for s in range(SUBLANES)]
            for q in range(SUBLANES)
        ]
        rows = solve_rows(pivot, rows)
        updated = []
        for t, tile in enumerate(tiles):
            if t == k:
                value = rows[0]
                for q in range(1, SUBLANES):
                    value = jnp.where(sublane == q, rows[q], value)
            else:
                value = tile
                for q in range(SUBLANES):
                    value = value - columns[t][q] * rows[q]
            updated.append(value)
        tiles = updated
    return jnp.concatenate([tile[:, n:] for tile in tiles], axis=0)


def inverse_kernel(*refs):
    count = (len(refs) - 1) // 2
    gram_refs, c_refs, out_ref = refs[:count], refs[count:-1], refs[-1]
    gram_c = total_of(c_refs)
    gram_b = total_of(gram_refs, 0, gram_c.shape[0])
    out_ref[...] = spd_inverse(unfold(gram_b * gram_c))


def inverse(grams_b, grams_c):
    rank = grams_c[0].shape[1] // 2
    return pl.pallas_call(
        inverse_kernel,
        out_shape=pltpu.VMEM((rank, rank), F32),
        in_specs=[VMEM] * (len(grams_b) + len(grams_c)),
        out_specs=VMEM,
        compiler_params=pltpu.CompilerParams(vmem_limit_bytes=4 << 20),
        cost_estimate=cost(4000000, 4000000),
        name="inverse",
    )(*grams_b, *grams_c)


def weigh(q_ref, factors, outs):
    row_block, rank, _ = q_ref.shape
    for tile in range(rank // SUBLANES):
        rows = pl.ds(tile * SUBLANES, SUBLANES)
        weights = [
            jnp.broadcast_to(
                factors[tile * SUBLANES : (tile + 1) * SUBLANES, i : i + 1], (SUBLANES, LANES)
            )
            for i in range(row_block)
        ]
        for out_ref, start, at, width in outs:
            for c in range(0, width, LANES):
                columns = pl.ds(pl.multiple_of(start + c, LANES), LANES)
                total = weights[0] * q_ref[0, rows, columns]
                for i in range(1, row_block):
                    total = total + weights[i] * q_ref[i, rows, columns]
                out_ref[rows, at + c : at + c + LANES] = total


def targets(q_ref, out_ref, shifts, other):
    side = lax.axis_index("ia") % 2
    side = 1 - side if other else side
    half = q_ref.shape[2] // 2
    width = half // lax.axis_size("ka")
    here = lax.axis_index("ka")
    return [
        (out_ref, side * half + (here ^ s) * width, n * width, width)
        for n, s in enumerate(shifts)
    ]


def solve_kernel(q_ref, inv_ref, *refs, shifts):
    sum_refs, (factors_ref, send_ref) = refs[:-2], refs[-2:]
    row_block, rank, _ = q_ref.shape
    packed = total_of(sum_refs)
    columns = []
    for tile in range(rank // SUBLANES):
        group, place = divmod(tile * row_block, LANES)
        columns.append(
            packed[group * SUBLANES : (group + 1) * SUBLANES, place : place + row_block]
        )
    factors = dot(inv_ref[...], jnp.concatenate(columns, axis=0), NN)
    factors_ref[...] = factors
    weigh(q_ref, factors, targets(q_ref, send_ref, shifts, True))


def row_kernel(factors_ref, out_ref):
    factors = factors_ref[...]
    mine = lax.axis_index("ja") * lax.axis_size("ka") + lax.axis_index("ka")
    lane = lax.broadcasted_iota(jnp.int32, factors.shape, 1)
    chosen = jnp.where(lane == mine, factors, 0.0)
    out_ref[...] = dot(jnp.ones((SUBLANES, factors.shape[1]), F32), chosen, NT)[:1, :]


def own_row(factors):
    return pl.pallas_call(
        row_kernel,
        out_shape=jax.ShapeDtypeStruct((1, factors.shape[0]), F32),
        in_specs=[VMEM],
        out_specs=VMEM,
        compiler_params=pltpu.CompilerParams(vmem_limit_bytes=2 << 20),
        name="own_row",
    )(factors)


def weigh_kernel(q_ref, factors_ref, out_ref, *, shifts, other):
    weigh(q_ref, factors_ref[...], targets(q_ref, out_ref, shifts, other))


def share(q, shifts):
    row_block, rank, width = q.shape
    columns = width // 2 // lax.axis_size("ka") * len(shifts)
    return (
        pltpu.VMEM((rank, columns), F32),
        cost(2 * row_block * rank * columns, 4 * row_block * rank * columns),
    )


def solve_and_weigh(q, inv, sums, shifts):
    row_block, rank, _ = q.shape
    shape, work = share(q, shifts)
    return pl.pallas_call(
        functools.partial(solve_kernel, shifts=shifts),
        out_shape=(pltpu.VMEM((rank, row_block), F32), shape),
        in_specs=[VMEM] * (2 + len(sums)),
        out_specs=[VMEM] * 2,
        compiler_params=pltpu.CompilerParams(vmem_limit_bytes=4 << 20),
        cost_estimate=work,
        name="solve",
    )(placed_in(q, pltpu.VMEM), inv, *sums)


def weigh_columns(q, factors, shifts, other):
    shape, work = share(q, shifts)
    return pl.pallas_call(
        functools.partial(weigh_kernel, shifts=shifts, other=other),
        out_shape=shape,
        in_specs=[VMEM] * 2,
        out_specs=VMEM,
        compiler_params=pltpu.CompilerParams(vmem_limit_bytes=4 << 20),
        cost_estimate=work,
        name="weigh",
    )(placed_in(q, pltpu.VMEM), factors)


def split_kernel(kept_ref, got_ref, *out_refs):
    width = out_refs[0].shape[1]
    for n, out_ref in enumerate(out_refs):
        columns = pl.ds(n * width, width)
        out_ref[...] = kept_ref[:, columns] + got_ref[:, columns]


def split_sums(kept, got, count):
    rank, columns = kept.shape
    return pl.pallas_call(
        split_kernel,
        out_shape=[pltpu.VMEM((rank, columns // count), F32)] * count,
        in_specs=[VMEM] * 2,
        out_specs=[VMEM] * count,
        compiler_params=pltpu.CompilerParams(vmem_limit_bytes=2 << 20),
        name="split_sums",
    )(kept, got)


def final_kernel(*refs):
    part_refs, out_ref = refs[:-1], refs[-1]
    out_ref[:, 0, :] = total_of(part_refs)


def final_sum(parts):
    rank, width = parts[0].shape
    return pl.pallas_call(
        final_kernel,
        out_shape=jax.ShapeDtypeStruct((rank, 1, width), F32),
        in_specs=[VMEM] * len(parts),
        out_specs=VMEM,
        compiler_params=pltpu.CompilerParams(vmem_limit_bytes=2 << 20),
        name="final_sum",
    )(*parts)


def swap(x, axis, s):
    n = lax.axis_size(axis)
    return lax.ppermute(x, axis, [(i, i ^ s) for i in range(n)])


def swaps(x, axis):
    n = lax.axis_size(axis)
    return [x] + [swap(x, axis, s) for s in range(1, n)]


def body(tensor, factor_b, factor_c):
    row_block, _, width = tensor.shape
    rank = factor_c.shape[1]
    n_ia, n_ka = lax.axis_size("ia"), lax.axis_size("ka")
    lines = row_block * rank // LANES
    bt = factor_b.T
    parts = swaps(bt, "ka")
    q, own_gram, gram_c = contract(tensor, bt, factor_c)
    grams_c = swaps(gram_c, "ka")
    sums = swaps(mode_one_sums(q, own_gram, parts), "ja")
    tails = swaps(add_tail(sums, lines), "ka")
    inv = inverse(sums, grams_c)
    if n_ia == 2 and width % (n_ia * n_ka * LANES) == 0:
        groups = chunks_of(n_ka)
        factors, sent = solve_and_weigh(q, inv, tails, groups[0])
        got = [swap(sent, "ia", 1)]
        for n, group in enumerate(groups[1:], 1):
            sent = weigh_columns(q, factors, group, True)
            got.append(swap(sent, "ia", 1))
        final = []
        for n, group in enumerate(groups):
            kept = weigh_columns(q, factors, group, False)
            pieces = split_sums(kept, got[n], len(group))
            final += [
                piece if s == 0 else swap(piece, "ka", s)
                for piece, s in zip(pieces, group)
            ]
        return own_row(factors), final_sum(final[::-1])
    factors, _ = solve_and_weigh(q, inv, tails, [0])
    whole = jnp.einsum("irj,ri->rj", q, factors, precision=HIGHEST)
    reduced = lax.psum_scatter(whole, ("ia", "ka"), scatter_dimension=1, tiled=True)
    return own_row(factors), reduced.reshape(rank, 1, reduced.shape[1])


def chunks_of(n_ka):
    return [[s] for s in reversed(range(2, n_ka))] + [[1, 0]]


def solution(mesh):
    placed = (P("ia", "ka", "ja"), P(("ja", "ka"), None), P("ka", None))
    return jax.shard_map(
        body,
        mesh=mesh,
        in_specs=placed,
        out_specs=(P(("ia", "ja", "ka"), None), P(None, "ja", ("ia", "ka"))),
        check_vma=False,
    )
```

```python
import functools

import jax
import jax.numpy as jnp
from jax import lax
from jax.experimental import pallas as pl
from jax.experimental.pallas import tpu as pltpu
from jax.sharding import PartitionSpec as P


F32 = jnp.float32
BF16 = jnp.bfloat16
HIGHEST = lax.Precision.HIGHEST
LANES = 128
SUBLANES = 8
VMEM = pl.BlockSpec(memory_space=pltpu.VMEM)
HBM = pl.BlockSpec(memory_space=pltpu.HBM)
NN = (((1,), (0,)), ((), ()))
NT = (((1,), (1,)), ((), ()))
TN = (((0,), (0,)), ((), ()))


def dot(a, b, dims):
    return lax.dot_general(a, b, dims, precision=HIGHEST, preferred_element_type=F32)


def cost(flops, bytes_accessed):
    return pl.CostEstimate(flops=flops, bytes_accessed=bytes_accessed, transcendentals=0)


def placed_in(x, space):
    return pltpu.with_memory_space_constraint(x, space)


def fold(square):
    half = square.shape[0] // 2
    return jnp.concatenate([square[:half, :], square[half:, :]], axis=1)


def unfold(folded):
    half = folded.shape[1] // 2
    return jnp.concatenate([folded[:, :half], folded[:, half:]], axis=0)


def total_of(refs, start=0, stop=None):
    total = refs[0][start:stop, :]
    for ref in refs[1:]:
        total = total + ref[start:stop, :]
    return total


def contract_kernel(
    x_hbm, b_hbm, c_hbm, q_ref, gram_b_ref, gram_c_ref, x_ref, b_ref, c_ref, lhs_ref, sems, *, chunks
):
    rows = q_ref.shape[0] // chunks
    copies = [
        pltpu.make_async_copy(
            x_hbm.at[pl.ds(n * rows, rows)], x_ref.at[pl.ds(n * rows, rows)], sems.at[n]
        )
        for n in range(chunks)
    ]
    c_copy = pltpu.make_async_copy(c_hbm, c_ref, sems.at[chunks])
    b_copy = pltpu.make_async_copy(b_hbm, b_ref, sems.at[chunks + 1])
    c_copy.start()
    b_copy.start()
    for copy in copies:
        copy.start()
    c_copy.wait()
    b_copy.wait()
    c = c_ref[...]
    gram_c_ref[...] = fold(dot(c, c, TN))
    gram_b_ref[...] = fold(gram_terms([b_ref], b_ref.shape[0]))
    ct = c.T
    high = ct.astype(BF16)
    low = (ct - high.astype(F32)).astype(BF16)
    lhs_ref[...] = jnp.concatenate([high, low, high, low], axis=1)
    for n, copy in enumerate(copies):
        copy.wait()
        for i in range(n * rows, (n + 1) * rows):
            x = x_ref[i]
            high = x.astype(BF16)
            low = (x - high.astype(F32)).astype(BF16)
            rhs = jnp.concatenate([high, high, low, low], axis=0)
            q_ref[i] = jnp.dot(lhs_ref[...], rhs, preferred_element_type=F32)


def contract(tensor, bt, factor_c):
    row_block, depth, width = tensor.shape
    rank = factor_c.shape[1]
    chunks = 4
    return pl.pallas_call(
        functools.partial(contract_kernel, chunks=chunks),
        out_shape=(
            pltpu.VMEM((row_block, rank, width), F32),
            pltpu.VMEM((rank // 2, 2 * rank), F32),
            pltpu.VMEM((rank // 2, 2 * rank), F32),
        ),
        in_specs=[HBM] * 3,
        out_specs=[VMEM] * 3,
        scratch_shapes=[
            pltpu.VMEM(tensor.shape, F32),
            pltpu.VMEM(bt.shape, F32),
            pltpu.VMEM(factor_c.shape, F32),
            pltpu.VMEM((rank, 4 * depth), BF16),
            pltpu.SemaphoreType.DMA((chunks + 2,)),
        ],
        compiler_params=pltpu.CompilerParams(vmem_limit_bytes=12 << 20),
        cost_estimate=cost(8 * row_block * depth * rank * width, 4 * row_block * depth * width),
        name="contract",
    )(*(placed_in(x, pltpu.HBM) for x in (tensor, bt, factor_c)))


def gram_terms(part_refs, rank):
    stacks = []
    for part in part_refs:
        value = part[:rank, :]
        first = value.astype(BF16)
        value = value - first.astype(F32)
        second = value.astype(BF16)
        third = (value - second.astype(F32)).astype(BF16)
        stacks.append(jnp.concatenate([first, second, third], axis=0))
    stack = jnp.concatenate(stacks, axis=1)
    terms = lax.dot_general(stack, stack, NT, preferred_element_type=F32)
    terms = terms[:, 2 * rank :] + terms[:, rank : 2 * rank] + terms[:, :rank]
    return terms[2 * rank :, :] + terms[rank : 2 * rank, :] + terms[:rank, :]


def weighted_sums(q_ref, part_refs, shifts):
    row_block, rank, _ = q_ref.shape
    width = part_refs[0].shape[1]
    here = lax.axis_index("ka")
    for tile in range(rank // SUBLANES):
        rows = pl.ds(tile * SUBLANES, SUBLANES)
        for i in range(row_block):
            total = None
            for s, part in zip(shifts, part_refs):
                start = (here ^ s) * width
                for c in range(0, width, LANES):
                    columns = pl.ds(pl.multiple_of(start + c, LANES), LANES)
                    term = q_ref[i, rows, columns] * part[rows, c : c + LANES]
                    total = term if total is None else total + term
            yield tile, i, total


def early_kernel(q_ref, own_ref, *refs, shifts):
    part_refs, (sums_ref, gram_ref) = refs[:-2], refs[-2:]
    row_block, rank, _ = q_ref.shape
    others = [part for s, part in zip(shifts, part_refs) if s != 0]
    gram_ref[...] = fold(gram_terms(others, rank)) + own_ref[...]
    for tile, i, total in weighted_sums(q_ref, part_refs, shifts):
        at = (tile * row_block + i) * SUBLANES
        sums_ref[at : at + SUBLANES, :] = total


def late_kernel(q_ref, sums_ref, gram_ref, *refs, shifts):
    part_refs, out_ref = refs[:-1], refs[-1]
    row_block, rank, _ = q_ref.shape
    half = rank // 2
    gram = fold(gram_terms(part_refs, rank))
    lane = lax.broadcasted_iota(jnp.int32, (SUBLANES, LANES), 1)
    groups = (out_ref.shape[0] - half) // SUBLANES
    packed = [jnp.zeros((SUBLANES, LANES), F32) for _ in range(groups)]
    for tile, i, total in weighted_sums(q_ref, part_refs, shifts):
        at = (tile * row_block + i) * SUBLANES
        total = total + sums_ref[at : at + SUBLANES, :]
        group, place = divmod(tile * row_block + i, LANES)
        packed[group] = jnp.where(
            lane == place, jnp.sum(total, axis=1, keepdims=True), packed[group]
        )
    for group, value in enumerate(packed):
        start = half + group * SUBLANES
        out_ref[start : start + SUBLANES, :] = value
    out_ref[:half, :] = gram + gram_ref[...]


def mode_one_sums(q, own_gram, parts):
    row_block, rank, width = q.shape
    lines = row_block * rank // LANES
    count = len(parts)
    split = set(range(count)) - {count - 1}
    early = [s for s in range(count) if s in split]
    late = [s for s in reversed(range(count)) if s not in split]
    params = pltpu.CompilerParams(vmem_limit_bytes=6 << 20)
    work = cost(row_block * rank * width, 2 * row_block * rank * width)
    q = placed_in(q, pltpu.VMEM)
    sums, gram = pl.pallas_call(
        functools.partial(early_kernel, shifts=early),
        out_shape=(
            pltpu.VMEM((row_block * rank, LANES), F32),
            pltpu.VMEM((rank // 2, 2 * rank), F32),
        ),
        in_specs=[VMEM] * (2 + len(early)),
        out_specs=[VMEM] * 2,
        compiler_params=params,
        cost_estimate=work,
        name="mode_one_early",
    )(q, own_gram, *[parts[s] for s in early])
    return pl.pallas_call(
        functools.partial(late_kernel, shifts=late),
        out_shape=pltpu.VMEM((rank // 2 + lines, LANES), F32),
        in_specs=[VMEM] * (3 + len(late)),
        out_specs=VMEM,
        compiler_params=params,
        cost_estimate=work,
        name="mode_one_late",
    )(q, sums, gram, *[parts[s] for s in late])


def add_kernel(*refs):
    part_refs, out_ref = refs[:-1], refs[-1]
    out_ref[...] = total_of(part_refs, part_refs[0].shape[0] - out_ref.shape[0])


def add_tail(parts, lines):
    return pl.pallas_call(
        add_kernel,
        out_shape=pltpu.VMEM((lines, LANES), F32),
        in_specs=[VMEM] * len(parts),
        out_specs=VMEM,
        compiler_params=pltpu.CompilerParams(vmem_limit_bytes=2 << 20),
        name="add_tail",
    )(*parts)


def solve_rows(pivot, rows):
    count = len(rows)
    rows = list(rows)
    block = {(q, s): pivot[q][s] for q in range(count) for s in range(q, count)}
    upper = {}
    for m in range(0, count, 2):
        a, b, d = block[m, m], block[m, m + 1], block[m + 1, m + 1]
        scale = 1.0 / (a * d - b * b)
        a, b, d = a * scale, b * scale, d * scale
        rows[m], rows[m + 1] = d * rows[m] - b * rows[m + 1], a * rows[m + 1] - b * rows[m]
        for s in range(m + 2, count):
            v, w = block[m, s], block[m + 1, s]
            upper[m, s], upper[m + 1, s] = d * v - b * w, a * w - b * v
        for q in range(m + 2, count):
            v, w = block[m, q], block[m + 1, q]
            for s in range(q, count):
                block[q, s] = block[q, s] - (v * upper[m, s] + w * upper[m + 1, s])
            rows[q] = rows[q] - (v * rows[m] + w * rows[m + 1])
    for m in range(count - 4, -1, -2):
        for s in range(m + 2, count):
            rows[m] = rows[m] - upper[m, s] * rows[s]
            rows[m + 1] = rows[m + 1] - upper[m + 1, s] * rows[s]
    return rows


def spd_inverse(matrix):
    n = matrix.shape[0]
    row = lax.broadcasted_iota(jnp.int32, (n, n), 0)
    column = lax.broadcasted_iota(jnp.int32, (n, n), 1)
    wide = jnp.concatenate([matrix, jnp.where(row == column, 1.0, 0.0).astype(F32)], axis=1)
    shape = (SUBLANES, 2 * n)
    tiles = [wide[t * SUBLANES : (t + 1) * SUBLANES, :] for t in range(n // SUBLANES)]
    sublane = lax.broadcasted_iota(jnp.int32, shape, 0)
    for k, block in enumerate(tiles):
        block = tiles[k]
        at = k * SUBLANES
        columns = [
            [jnp.broadcast_to(tile[:, at + q : at + q + 1], shape) for q in range(SUBLANES)]
            for tile in tiles
        ]
        rows = [jnp.broadcast_to(block[q : q + 1, :], shape) for q in range(SUBLANES)]
        pivot = [
            [jnp.broadcast_to(columns[k][s][q : q + 1, :], shape) for s in range(SUBLANES)]
            for q in range(SUBLANES)
        ]
        rows = solve_rows(pivot, rows)
        updated = []
        for t, tile in enumerate(tiles):
            if t == k:
                value = rows[0]
                for q in range(1, SUBLANES):
                    value = jnp.where(sublane == q, rows[q], value)
            else:
                value = tile
                for q in range(SUBLANES):
                    value = value - columns[t][q] * rows[q]
            updated.append(value)
        tiles = updated
    return jnp.concatenate([tile[:, n:] for tile in tiles], axis=0)


def inverse_kernel(*refs):
    count = (len(refs) - 1) // 2
    gram_refs, c_refs, out_ref = refs[:count], refs[count:-1], refs[-1]
    gram_c = total_of(c_refs)
    gram_b = total_of(gram_refs, 0, gram_c.shape[0])
    out_ref[...] = spd_inverse(unfold(gram_b * gram_c))


def inverse(grams_b, grams_c):
    rank = grams_c[0].shape[1] // 2
    return pl.pallas_call(
        inverse_kernel,
        out_shape=pltpu.VMEM((rank, rank), F32),
        in_specs=[VMEM] * (len(grams_b) + len(grams_c)),
        out_specs=VMEM,
        compiler_params=pltpu.CompilerParams(vmem_limit_bytes=4 << 20),
        cost_estimate=cost(4000000, 4000000),
        name="inverse",
    )(*grams_b, *grams_c)


def weigh(q_ref, weight_of, outs):
    row_block, rank, _ = q_ref.shape
    for tile in range(rank // SUBLANES):
        rows = pl.ds(tile * SUBLANES, SUBLANES)
        weights = [weight_of(tile, i) for i in range(row_block)]
        for out_ref, start, at, width in outs:
            for c in range(0, width, LANES):
                columns = pl.ds(pl.multiple_of(start + c, LANES), LANES)
                total = weights[0] * q_ref[0, rows, columns]
                for i in range(1, row_block):
                    total = total + weights[i] * q_ref[i, rows, columns]
                out_ref[rows, at + c : at + c + LANES] = total


def weight_rows(tile, i, row_block):
    at = (tile * row_block + i) * SUBLANES
    return slice(at, at + SUBLANES)


def targets(q_ref, out_ref, shifts, other):
    side = lax.axis_index("ia") % 2
    side = 1 - side if other else side
    half = q_ref.shape[2] // 2
    width = half // lax.axis_size("ka")
    here = lax.axis_index("ka")
    return [
        (out_ref, side * half + (here ^ s) * width, n * width, width)
        for n, s in enumerate(shifts)
    ]


def solve_kernel(q_ref, inv_ref, *refs, shifts):
    sum_refs, (factors_ref, weights_ref, send_ref) = refs[:-3], refs[-3:]
    row_block, rank, _ = q_ref.shape
    packed = total_of(sum_refs)
    columns = []
    for tile in range(rank // SUBLANES):
        group, place = divmod(tile * row_block, LANES)
        columns.append(
            packed[group * SUBLANES : (group + 1) * SUBLANES, place : place + row_block]
        )
    factors = dot(inv_ref[...], jnp.concatenate(columns, axis=0), NN)
    factors_ref[...] = factors

    def weight_of(tile, i):
        rows = slice(tile * SUBLANES, (tile + 1) * SUBLANES)
        weight = jnp.broadcast_to(factors[rows, i : i + 1], (SUBLANES, LANES))
        weights_ref[weight_rows(tile, i, row_block), :] = weight
        return weight

    weigh(q_ref, weight_of, targets(q_ref, send_ref, shifts, True))


def row_kernel(factors_ref, out_ref):
    factors = factors_ref[...]
    mine = lax.axis_index("ja") * lax.axis_size("ka") + lax.axis_index("ka")
    lane = lax.broadcasted_iota(jnp.int32, factors.shape, 1)
    chosen = jnp.where(lane == mine, factors, 0.0)
    out_ref[...] = dot(jnp.ones((SUBLANES, factors.shape[1]), F32), chosen, NT)[:1, :]


def own_row(factors):
    return pl.pallas_call(
        row_kernel,
        out_shape=jax.ShapeDtypeStruct((1, factors.shape[0]), F32),
        in_specs=[VMEM],
        out_specs=VMEM,
        compiler_params=pltpu.CompilerParams(vmem_limit_bytes=2 << 20),
        name="own_row",
    )(factors)


def weigh_kernel(q_ref, weights_ref, out_ref, *, shifts, other):
    def weight_of(tile, i):
        return weights_ref[weight_rows(tile, i, q_ref.shape[0]), :]

    weigh(q_ref, weight_of, targets(q_ref, out_ref, shifts, other))


def share(q, shifts):
    row_block, rank, width = q.shape
    columns = width // 2 // lax.axis_size("ka") * len(shifts)
    return (
        pltpu.VMEM((rank, columns), F32),
        cost(2 * row_block * rank * columns, 4 * row_block * rank * columns),
    )


def solve_and_weigh(q, inv, sums, shifts):
    row_block, rank, _ = q.shape
    shape, work = share(q, shifts)
    return pl.pallas_call(
        functools.partial(solve_kernel, shifts=shifts),
        out_shape=(
            pltpu.VMEM((rank, row_block), F32),
            pltpu.VMEM((rank * row_block, LANES), F32),
            shape,
        ),
        in_specs=[VMEM] * (2 + len(sums)),
        out_specs=[VMEM] * 3,
        compiler_params=pltpu.CompilerParams(vmem_limit_bytes=4 << 20),
        cost_estimate=work,
        name="solve",
    )(placed_in(q, pltpu.VMEM), inv, *sums)


def weigh_columns(q, weights, shifts, other):
    shape, work = share(q, shifts)
    return pl.pallas_call(
        functools.partial(weigh_kernel, shifts=shifts, other=other),
        out_shape=shape,
        in_specs=[VMEM] * 2,
        out_specs=VMEM,
        compiler_params=pltpu.CompilerParams(vmem_limit_bytes=4 << 20),
        cost_estimate=work,
        name="weigh",
    )(placed_in(q, pltpu.VMEM), weights)


def split_kernel(kept_ref, got_ref, *out_refs):
    width = out_refs[0].shape[1]
    for n, out_ref in enumerate(out_refs):
        columns = pl.ds(n * width, width)
        out_ref[...] = kept_ref[:, columns] + got_ref[:, columns]


def split_sums(kept, got, count):
    rank, columns = kept.shape
    return pl.pallas_call(
        split_kernel,
        out_shape=[pltpu.VMEM((rank, columns // count), F32)] * count,
        in_specs=[VMEM] * 2,
        out_specs=[VMEM] * count,
        compiler_params=pltpu.CompilerParams(vmem_limit_bytes=2 << 20),
        name="split_sums",
    )(kept, got)


def final_kernel(*refs):
    part_refs, out_ref = refs[:-1], refs[-1]
    out_ref[:, 0, :] = total_of(part_refs)


def final_sum(parts):
    rank, width = parts[0].shape
    return pl.pallas_call(
        final_kernel,
        out_shape=jax.ShapeDtypeStruct((rank, 1, width), F32),
        in_specs=[VMEM] * len(parts),
        out_specs=VMEM,
        compiler_params=pltpu.CompilerParams(vmem_limit_bytes=2 << 20),
        name="final_sum",
    )(*parts)


def swap(x, axis, s):
    n = lax.axis_size(axis)
    return lax.ppermute(x, axis, [(i, i ^ s) for i in range(n)])


def swaps(x, axis):
    n = lax.axis_size(axis)
    return [x] + [swap(x, axis, s) for s in range(1, n)]


def crossed(x):
    n_ja, n_ka = lax.axis_size("ja"), lax.axis_size("ka")
    got = [x]
    for s in range(1, n_ka):
        pairs = [(i, i ^ (n_ka + s)) for i in range(n_ja * n_ka)]
        got.append(lax.ppermute(x, ("ja", "ka"), pairs))
    return got


def body(tensor, factor_b, factor_c):
    row_block, _, width = tensor.shape
    rank = factor_c.shape[1]
    n_ia, n_ka = lax.axis_size("ia"), lax.axis_size("ka")
    lines = row_block * rank // LANES
    bt = factor_b.T
    parts = swaps(bt, "ka")
    q, own_gram, gram_c = contract(tensor, bt, factor_c)
    grams_c = swaps(gram_c, "ka")
    sums = swaps(mode_one_sums(q, own_gram, parts), "ja")
    tails = crossed(add_tail(sums, lines))
    inv = inverse(sums, grams_c)
    if n_ia == 2 and width % (n_ia * n_ka * LANES) == 0:
        groups = chunks_of(n_ka)
        factors, weights, sent = solve_and_weigh(q, inv, tails, groups[0])
        got = [swap(sent, "ia", 1)]
        for n, group in enumerate(groups[1:], 1):
            sent = weigh_columns(q, weights, group, True)
            got.append(swap(sent, "ia", 1))
        final = []
        for n, group in enumerate(groups):
            kept = weigh_columns(q, weights, group, False)
            pieces = split_sums(kept, got[n], len(group))
            final += [
                piece if s == 0 else swap(piece, "ka", s)
                for piece, s in zip(pieces, group)
            ]
        return own_row(factors), final_sum(final[::-1])
    factors, _, _ = solve_and_weigh(q, inv, tails, [0])
    whole = jnp.einsum("irj,ri->rj", q, factors, precision=HIGHEST)
    reduced = lax.psum_scatter(whole, ("ia", "ka"), scatter_dimension=1, tiled=True)
    return own_row(factors), reduced.reshape(rank, 1, reduced.shape[1])


def chunks_of(n_ka):
    return [[s] for s in reversed(range(2, n_ka))] + [[1, 0]]


def solution(mesh):
    placed = (P("ia", "ka", "ja"), P(("ja", "ka"), None), P("ka", None))
    return jax.shard_map(
        body,
        mesh=mesh,
        in_specs=placed,
        out_specs=(P(("ia", "ja", "ka"), None), P(None, "ja", ("ia", "ka"))),
        check_vma=False,
    )
```
